32 devices in a mesh: occ: 2 (over core), vir: 16 (over z, y, x).
Axes of the slice: x: 2, y: 2, z: 4, core: 2. Of those that a mesh axis runs over, the one named last changes fastest.
Arguments:
- amplitudes: bfloat16 [2256, 6144], P('occ', 'vir'), may hold values from -6 to 6
- ladder_ints: bfloat16 [6144, 6144], P('vir', 'occ'), as said below
- tile_map: int32 [48, 48], replicated, may hold values from 0 to 1, as said below
- hole_ints: bfloat16 [2256, 2256], P('occ'), may hold values from -0.125 to 0.125
- occ_energy: float32 [48], replicated, may hold values from -2 to -0.3
- pair_list: int32 [2256, 2], P('occ'), may hold values from 0 to 47, as said below
- mirror_row: int32 [2256], P('occ'), may hold values from 0 to 2255, as said below
Outputs:
- residual: float32 [2256, 6144], P('occ', 'vir')
The draws below stay inside these ranges and needn't reach their ends.
Inputs may be any that keep to these rules, and one draw needn't show every extreme that they name: symmetric: ladder_ints[ab, cd] equals ladder_ints[cd, ab]. `tile_map`: symmetric. `pair_list`: each ordered pair of distinct orbitals of the 48 occupied ones stands in exactly one row. Row mirror_row[r] holds the pair of row r reversed.
All inputs are finite; a program needn't handle non-finite values.
Results may differ from the reference program's by a relative error of at most 0.0003.
Values may be sent and summed in bfloat16 or wider, within the bound.
No kernel may reach another device: no remote copies, remote signals or barrier semaphores. Data moves between devices by JAX's collectives and lax.ppermute only.
A program may use at most 64 MiB of HBM per device.

```python
import math
import jax
import jax.numpy as jnp

NOCC = 48
TILE = 128
OCC_PAIRS = 2256
VPAIRS = 6144
NTILES = 48


def draw_ladder_ints(key, part):
    noise = jax.random.normal(jax.random.fold_in(key, 5), (VPAIRS, VPAIRS), jnp.float32)
    symmetric = (noise + noise.T) * (1.0 / math.sqrt(VPAIRS))
    return symmetric.astype(jnp.bfloat16)


def draw_tile_map(key, part):
    coins = jax.random.randint(jax.random.fold_in(key, 11), (NTILES, NTILES), 0, 2).astype(jnp.int32)
    return (jnp.triu(coins) + jnp.triu(coins, 1).T).astype(jnp.int32)


def pair_order(key):
    return jax.random.permutation(jax.random.fold_in(key, 23), OCC_PAIRS).astype(jnp.int32)


def pair_members(order):
    first = order // (NOCC - 1)
    others = order % (NOCC - 1)
    second = others + (others >= first).astype(jnp.int32)
    return (first.astype(jnp.int32), second.astype(jnp.int32))


def draw_pair_list(key, part):
    first, second = pair_members(pair_order(key))
    return jnp.stack([first, second], axis=1).astype(jnp.int32)


def draw_mirror_row(key, part):
    order = pair_order(key)
    first, second = pair_members(order)
    canonical = second * (NOCC - 1) + first - (first > second).astype(jnp.int32)
    position = jnp.zeros((OCC_PAIRS,), jnp.int32).at[order].set(jnp.arange(OCC_PAIRS, dtype=jnp.int32))
    return position[canonical].astype(jnp.int32)


def steps_of(stream_key, dims, cuts, low, largest):
    gain = 1.0
    for dim, parts in cuts:
        heights = jax.random.uniform(jax.random.fold_in(jax.random.fold_in(stream_key, 6), dim), (parts,), jnp.float32, low / len(cuts), largest / len(cuts))
        gain = gain * jnp.repeat(jnp.exp(heights), dims[dim] // parts).reshape((-1,) + (1,) * (len(dims) - 1 - dim))
    return gain


def scatter_about(stream_key, dims, deviation, most, shards=(), held_as=jnp.bfloat16):
    entries = jax.random.normal(stream_key, dims, jnp.float32) * deviation
    if len(shards) > 0:
        entries = steps_of(stream_key, dims, shards, -0.22, 0.18) * entries
    return jnp.clip(entries, min=-most, max=most).astype(held_as)


def setup_inputs(seed: int = 0) -> dict:
    keys = jax.random.split(jax.random.key(seed), 8)
    return {
        "amplitudes": scatter_about(keys[0], (OCC_PAIRS, VPAIRS), 1.0, 6.0, ((0, 2), (1, 16))),
        "ladder_ints": draw_ladder_ints(jax.random.fold_in(keys[7], 71), 0),
        "tile_map": draw_tile_map(jax.random.fold_in(keys[7], 71), 0),
        "hole_ints": scatter_about(keys[3], (OCC_PAIRS, OCC_PAIRS), OCC_PAIRS ** -0.5, 0.125, ((0, 2),)),
        "occ_energy": jnp.clip(jax.random.uniform(keys[4], (NOCC,), jnp.float32, -2.0, -0.3), -2.0, -0.3),
        "pair_list": draw_pair_list(jax.random.fold_in(keys[7], 71), 0),
        "mirror_row": draw_mirror_row(jax.random.fold_in(keys[7], 71), 0),
    }


def reference(amplitudes, ladder_ints, tile_map, hole_ints, occ_energy, pair_list, mirror_row):
    tile_mask = jnp.kron(tile_map.astype(jnp.float32), jnp.ones((TILE, TILE), jnp.float32)).astype(ladder_ints.dtype)
    masked = ladder_ints * tile_mask
    ladder = jnp.dot(amplitudes, masked.T, preferred_element_type=jnp.float32)
    hole = jnp.dot(hole_ints, amplitudes, preferred_element_type=jnp.float32)
    pair_energy = occ_energy[pair_list[:, 0]] + occ_energy[pair_list[:, 1]]
    raw = ladder + hole - pair_energy[:, None] * amplitudes.astype(jnp.float32)
    mirrored = raw[mirror_row]
    swapped = mirrored.reshape(OCC_PAIRS, VPAIRS // 2, 2)[:, :, ::-1].reshape(OCC_PAIRS, VPAIRS)
    return raw + swapped
```

```python
import functools

import jax
import jax.numpy as jnp
from jax import lax
from jax.experimental import pallas as pl
from jax.experimental.pallas import tpu as pltpu
from jax.sharding import PartitionSpec as P

TILE = 128
CHUNKS = 2


def row_chunks(rows, count):
    step = -(-rows // (count * 16)) * 16
    starts = list(range(0, rows, step))
    return [(start, min(step, rows - start)) for start in starts]


def other_core(a):
    return lax.ppermute(a, "occ", [(0, 1), (1, 0)])


def mirror_kernel(offsets, index_ref, own_ref, *refs):
    *pieces, out_ref, whole, picked, sems = refs
    copies = []
    for k, (piece, offset) in enumerate(zip(pieces, offsets)):
        copy = pltpu.make_async_copy(piece, whole.at[pl.ds(offset, piece.shape[0])], sems.at[k])
        copy.start()
        copies.append(copy)
    for copy in copies:
        copy.wait()
    rows, cols = own_ref.shape
    group = 8

    def pick(g, carry):
        for j in range(group):
            r = g * group + j
            picked[pl.ds(r, 1), :] = whole[pl.ds(index_ref[r], 1), :]
        return carry

    lax.fori_loop(0, rows // group, pick, 0)
    for r in range(rows // group * group, rows):
        picked[pl.ds(r, 1), :] = whole[pl.ds(index_ref[r], 1), :]

    odd = lax.broadcasted_iota(jnp.int32, (rows, TILE), 1) % 2 == 1
    for c in range(0, cols, TILE):
        part = picked[:, c : c + TILE]
        swapped = jnp.where(odd, pltpu.roll(part, 1, 1), pltpu.roll(part, TILE - 1, 1))
        out_ref[:, c : c + TILE] = own_ref[:, c : c + TILE] + swapped


def add_mirror(index, own, pieces):
    rows, cols = own.shape
    offsets = []
    total = 0
    for piece in pieces:
        offsets.append(total)
        total += piece.shape[0]
    return pl.pallas_call(
        functools.partial(mirror_kernel, tuple(offsets)),
        out_shape=jax.ShapeDtypeStruct((rows, cols), jnp.float32),
        in_specs=[
            pl.BlockSpec(memory_space=pltpu.SMEM),
            pl.BlockSpec(memory_space=pltpu.VMEM),
        ]
        + [pl.BlockSpec(memory_space=pl.ANY)] * len(pieces),
        out_specs=pl.BlockSpec(memory_space=pltpu.VMEM),
        scratch_shapes=[
            pltpu.VMEM((total, cols), jnp.float32),
            pltpu.VMEM((rows, cols), jnp.float32),
            pltpu.SemaphoreType.DMA((len(pieces),)),
        ],
        cost_estimate=pl.CostEstimate(
            flops=rows * cols, bytes_accessed=(total + 2 * rows) * cols * 4, transcendentals=0
        ),
        name="mirror",
    )(index, own, *pieces)


def shards(cores, chips, amplitudes, ladder_ints, tile_map, hole_ints, occ_energy, pair_list, mirror_row):
    rows, cols = amplitudes.shape
    integral_cols = ladder_ints.shape[1]
    vir_place = lax.axis_index("vir")
    occ_place = lax.axis_index("occ")
    row_tiles = cols // TILE
    col_tiles = integral_cols // TILE
    members = chips // 2
    half_blocks = integral_cols // cols // 2
    side = vir_place % 2
    group = vir_place // 2
    across = [(v, v ^ 1) for v in range(chips)]

    order = list(range(0, members, 2)) + list(range(members - 1 - members % 2, 0, -2))
    place_of = [order.index(g) for g in range(members)]
    place = jnp.array(place_of, jnp.int32)[group]
    order_arr = jnp.array(order, jnp.int32)
    forward, backward = [], []
    for s in range(2):
        for k in range(members):
            here, there = 2 * order[k] + s, 2 * order[(k + 1) % members] + s
            forward.append((here, there))
            backward.append((there, here))

    tile_block = lax.dynamic_slice(
        tile_map, (vir_place * row_tiles, occ_place * col_tiles), (row_tiles, col_tiles)
    )
    tile_mask = jnp.broadcast_to(tile_block[:, None, :, None], (row_tiles, TILE, col_tiles, TILE))
    masked = ladder_ints * tile_mask.reshape(cols, integral_cols).astype(ladder_ints.dtype)

    def of_side(which):
        return jnp.concatenate(
            [
                lax.dynamic_slice(masked, (0, (2 * j + which) * cols), (cols, cols))
                for j in range(half_blocks)
            ],
            axis=1,
        )

    kept = of_side(side)
    near = lax.ppermute(of_side(1 - side), "vir", across)

    def whole_k(a):
        if cores == 2:
            return jnp.concatenate([a, other_core(a)], axis=1)
        return lax.all_gather(a, "occ", axis=1, tiled=True)

    kept_all = whole_k(kept)
    near_all = whole_k(near)
    first_block = occ_place * half_blocks if cores == 2 else 0

    def k_block(v_all, step):
        g = order_arr[(place - step) % members]
        at = (g - first_block) % members
        return lax.dynamic_slice(v_all, (0, at * cols), (cols, cols))

    if cores == 2:
        both = jnp.zeros((2 * rows, cols), amplitudes.dtype)
        both = lax.dynamic_update_slice(both, amplitudes, (occ_place * rows, 0))
        both = lax.dynamic_update_slice(both, other_core(amplitudes), ((1 - occ_place) * rows, 0))
    else:
        both = lax.all_gather(amplitudes, "occ", axis=0, tiled=True)
    orbital_ids = jnp.arange(occ_energy.shape[0], dtype=jnp.int32)
    one_hot = (pair_list[:, :, None] == orbital_ids[None, None, :]).astype(jnp.float32)
    pair_energy = jnp.sum(one_hot * occ_energy[None, None, :], axis=(1, 2))
    base = jnp.dot(hole_ints, both, preferred_element_type=jnp.float32)
    base = base - pair_energy[:, None] * amplitudes.astype(jnp.float32)

    chunks = row_chunks(rows, CHUNKS)
    raws = []
    for index, (start, length) in enumerate(chunks):
        mine = amplitudes[start : start + length]
        blocks = {0: mine}
        ups = members // 2 if index % 2 == 0 else (members - 1) // 2
        travelling = mine
        for step in range(1, ups + 1):
            travelling = lax.ppermute(travelling, "vir", forward)
            blocks[step] = travelling
        travelling = mine
        for step in range(1, members - ups):
            travelling = lax.ppermute(travelling, "vir", backward)
            blocks[-step] = travelling

        def product(v_all):
            total = None
            for step, block in blocks.items():
                term = lax.dot_general(
                    block,
                    k_block(v_all, step),
                    (((1,), (1,)), ((), ())),
                    preferred_element_type=jnp.float32,
                )
                total = term if total is None else total + term
            return total

        from_near = lax.ppermute(product(near_all), "vir", across)
        raws.append(base[start : start + length] + product(kept_all) + from_near)

    own = jnp.concatenate(raws, axis=0)
    if cores == 2:
        pieces = raws + [other_core(raw) for raw in raws]
        index = (mirror_row - occ_place * rows) % (2 * rows)
    else:
        pieces = [lax.all_gather(own, "occ", axis=0, tiled=True)]
        index = mirror_row
    return add_mirror(index, own, pieces)


def solution(mesh):
    body = functools.partial(shards, mesh.shape["occ"], mesh.shape["vir"])
    return jax.shard_map(
        body,
        mesh=mesh,
        in_specs=(
            P("occ", "vir"),
            P("vir", "occ"),
            P(),
            P("occ", None),
            P(),
            P("occ", None),
            P("occ"),
        ),
        out_specs=P("occ", "vir"),
        check_vma=False,
    )
```

```python
import functools

import jax
import jax.numpy as jnp
from jax import lax
from jax.experimental import pallas as pl
from jax.experimental.pallas import tpu as pltpu
from jax.sharding import PartitionSpec as P


TILE = 128
CHUNKS = 4


LIMIT = 16 * 1024 * 1024

SMEM = pl.BlockSpec(memory_space=pltpu.SMEM)
VMEM = pl.BlockSpec(memory_space=pltpu.VMEM)
ANY = pl.BlockSpec(memory_space=pl.ANY)


def row_chunks(rows, count):
    step = -(-rows // (count * 8)) * 8
    starts = list(range(0, rows, step))
    return [(start, min(step, rows - start)) for start in starts]


def other_core(a):
    return lax.ppermute(a, "occ", [(0, 1), (1, 0)])


def rows_kernel(chunks, a_ref, *refs):
    for (start, length), out in zip(chunks, refs):
        out[...] = a_ref[start : start + length, :]


def split_rows(a, chunks):
    return pl.pallas_call(
        functools.partial(rows_kernel, chunks),
        out_shape=[jax.ShapeDtypeStruct((length, a.shape[1]), a.dtype) for _, length in chunks],
        in_specs=[VMEM],
        out_specs=[VMEM] * len(chunks),
        compiler_params=pltpu.CompilerParams(vmem_limit_bytes=LIMIT),
        cost_estimate=pl.CostEstimate(flops=0, bytes_accessed=2 * a.size * 2, transcendentals=0),
        name="split_rows",
    )(a)


def sides_kernel(where_ref, map_ref, v_ref, send_ref, kept_ref):
    side, first_row, first_col = where_ref[0], where_ref[1], where_ref[2]
    cols = v_ref.shape[0]
    tiles = cols // TILE
    for out, which in ((send_ref, 1 - side), (kept_ref, side)):
        for j in range(out.shape[1] // cols):
            block = 2 * j + which
            for r in range(tiles):
                for c in range(tiles):
                    allowed = map_ref[first_row + r, first_col + block * tiles + c]
                    at = pl.multiple_of(block * cols + c * TILE, TILE)
                    tile = v_ref[r * TILE : (r + 1) * TILE, pl.ds(at, TILE)]
                    out[r * TILE : (r + 1) * TILE, j * cols + c * TILE : j * cols + (c + 1) * TILE] = (
                        jnp.where(allowed == 1, tile, jnp.zeros_like(tile))
                    )


def split_sides(where, tile_map, integrals):
    cols, width = integrals.shape
    half = jax.ShapeDtypeStruct((cols, width // 2), integrals.dtype)
    return pl.pallas_call(
        sides_kernel,
        out_shape=[half, half],
        in_specs=[SMEM, SMEM, VMEM],
        out_specs=[VMEM, VMEM],
        compiler_params=pltpu.CompilerParams(vmem_limit_bytes=LIMIT),
        cost_estimate=pl.CostEstimate(
            flops=integrals.size, bytes_accessed=4 * integrals.size, transcendentals=0
        ),
        name="split_sides",
    )(where, tile_map, integrals)


def product_kernel(count, parts, start, at_ref, *refs):
    blocks, pieces = refs[:count], refs[count : count + parts]
    addend = refs[count + parts] if start is not None else None
    out_ref, piece_buf, sems = refs[-3:]
    length, cols = out_ref.shape
    per_piece = pieces[0].shape[1] // cols

    def piece_copy(k, p, at):
        return pltpu.make_async_copy(
            pieces[p].at[:, pl.ds(pl.multiple_of(at * cols, cols), cols)], piece_buf.at[k], sems.at[k]
        )

    for k in range(count):
        for p in range(parts):
            at = at_ref[k] - p * per_piece

            @pl.when((at >= 0) & (at < per_piece))
            def _():
                piece_copy(k, p, at).start()

    for k in range(count):
        piece_copy(k, 0, 0).wait()
        term = lax.dot_general(
            blocks[k][...], piece_buf[k], (((1,), (1,)), ((), ())), preferred_element_type=jnp.float32
        )
        if k > 0:
            out_ref[...] += term
        elif start is not None:
            out_ref[...] = term + addend[start : start + length, :]
        else:
            out_ref[...] = term


def product(at, blocks, pieces, addend=None, start=None):
    count, parts = len(blocks), len(pieces)
    length, cols = blocks[0].shape
    given = [addend] if start is not None else []
    return pl.pallas_call(
        functools.partial(product_kernel, count, parts, start),
        out_shape=jax.ShapeDtypeStruct((length, cols), jnp.float32),
        in_specs=[SMEM] + [VMEM] * (count + parts + len(given)),
        out_specs=VMEM,
        scratch_shapes=[
            pltpu.VMEM((count, cols, cols), jnp.bfloat16),
            pltpu.SemaphoreType.DMA((count,)),
        ],
        compiler_params=pltpu.CompilerParams(vmem_limit_bytes=LIMIT),
        cost_estimate=pl.CostEstimate(
            flops=2 * count * length * cols * cols,
            bytes_accessed=2 * count * (length + cols) * cols + 4 * length * cols,
            transcendentals=0,
        ),
        name="product",
    )(at, *blocks, *pieces, *given)


def mirror_kernel(offsets, index_ref, *refs):
    *pieces, out_ref, whole, sems = refs
    copies = []
    for k, offset in enumerate(offsets):
        copy = pltpu.make_async_copy(
            pieces[k], whole.at[pl.ds(offset, pieces[k].shape[0])], sems.at[k]
        )
        copy.start()
        copies.append(copy)
    for copy in copies:
        copy.wait()
    rows, cols = out_ref.shape
    odd = lax.broadcasted_iota(jnp.int32, (8, TILE), 1) % 2 == 1

    def group(start, size):
        picked = jnp.concatenate(
            [whole[pl.ds(index_ref[start + j], 1), :] for j in range(size)], axis=0
        )
        for c in range(0, cols, TILE):
            part = picked[:, c : c + TILE]
            swapped = jnp.where(odd[:size], pltpu.roll(part, 1, 1), pltpu.roll(part, TILE - 1, 1))
            out_ref[pl.ds(start, size), c : c + TILE] = (
                whole[pl.ds(start, size), c : c + TILE] + swapped
            )

    def step(g, carry):
        group(pl.multiple_of(g * 8, 8), 8)
        return carry

    lax.fori_loop(0, rows // 8, step, 0)
    if rows % 8:
        group(rows // 8 * 8, rows % 8)


def add_mirror(index, rows, pieces):
    cols = pieces[0].shape[1]
    offsets, total = [], 0
    for piece in pieces:
        offsets.append(total)
        total += -(-piece.shape[0] // 8) * 8
    return pl.pallas_call(
        functools.partial(mirror_kernel, tuple(offsets)),
        out_shape=jax.ShapeDtypeStruct((rows, cols), jnp.float32),
        in_specs=[SMEM] + [ANY] * len(pieces),
        out_specs=VMEM,
        scratch_shapes=[
            pltpu.VMEM((total, cols), jnp.float32),
            pltpu.SemaphoreType.DMA((len(pieces),)),
        ],
        compiler_params=pltpu.CompilerParams(vmem_limit_bytes=LIMIT),
        cost_estimate=pl.CostEstimate(
            flops=rows * cols, bytes_accessed=(total + rows) * cols * 4, transcendentals=0
        ),
        name="mirror",
    )(index, *pieces)


def shards(cores, chips, amplitudes, ladder_ints, tile_map, hole_ints, occ_energy, pair_list, mirror_row):
    rows, cols = amplitudes.shape
    integral_cols = ladder_ints.shape[1]
    vir_place = lax.axis_index("vir")
    occ_place = lax.axis_index("occ")
    members = chips // 2
    half_blocks = integral_cols // cols // 2
    side = vir_place % 2
    group = vir_place // 2
    across = [(v, v ^ 1) for v in range(chips)]

    evens = (members + 1) // 2
    order = [2 * p if p < evens else 2 * (members - p) - 1 for p in range(members)]
    forward, backward = [], []
    for s in range(2):
        for k in range(members):
            here, there = 2 * order[k] + s, 2 * order[(k + 1) % members] + s
            forward.append((here, there))
            backward.append((there, here))
    place = jnp.where(group % 2 == 0, group // 2, members - (group + 1) // 2)
    own_half = occ_place * half_blocks if cores == 2 else 0

    def positions(steps):
        p = (place - jnp.array(steps, jnp.int32)) % members
        g = jnp.where(p < evens, 2 * p, 2 * (members - p) - 1)
        return (g - own_half) % members

    def whole_k(a):
        if cores == 2:
            return [a, other_core(a)]
        return [lax.all_gather(a, "occ", axis=1, tiled=True)]

    chunks = row_chunks(rows, CHUNKS)
    mine = split_rows(amplitudes, chunks)

    where = jnp.stack([side, vir_place * (cols // TILE), occ_place * (integral_cols // TILE)])
    send, kept = split_sides(where.astype(jnp.int32), tile_map, ladder_ints)
    near = lax.ppermute(send, "vir", across)
    kept_all = whole_k(kept)
    near_all = whole_k(near)

    if cores == 2:
        both = jnp.zeros((2 * rows, cols), amplitudes.dtype)
        both = lax.dynamic_update_slice(both, amplitudes, (occ_place * rows, 0))
        both = lax.dynamic_update_slice(both, other_core(amplitudes), ((1 - occ_place) * rows, 0))
    else:
        both = lax.all_gather(amplitudes, "occ", axis=0, tiled=True)
    orbital_ids = jnp.arange(occ_energy.shape[0], dtype=jnp.int32)
    one_hot = (pair_list[:, :, None] == orbital_ids[None, None, :]).astype(jnp.float32)
    pair_energy = jnp.sum(one_hot * occ_energy[None, None, :], axis=(1, 2))
    base = jnp.dot(hole_ints, both, preferred_element_type=jnp.float32)
    base = base - pair_energy[:, None] * amplitudes.astype(jnp.float32)

    raws = []
    for index, (start, length) in enumerate(chunks):
        ups = members // 2 if index % 2 == 0 else (members - 1) // 2
        blocks = {0: mine[index]}
        for step in range(1, ups + 1):
            blocks[step] = lax.ppermute(blocks[step - 1], "vir", forward)
        for step in range(1, members - ups):
            blocks[-step] = lax.ppermute(blocks[1 - step], "vir", backward)
        steps = sorted(blocks, key=abs)
        at = positions(steps)
        arrived = [blocks[s] for s in steps]
        for_near = product(at, arrived, near_all)
        from_near = lax.ppermute(for_near, "vir", across)
        rest = product(at, arrived, kept_all, base, start)
        raws.append(rest + from_near)

    if cores == 2:
        pieces = raws + [other_core(raw) for raw in raws]
        index = (mirror_row - occ_place * rows) % (2 * rows)
        return add_mirror(index, rows, pieces)
    own = jnp.concatenate(raws, axis=0)
    whole = lax.all_gather(own, "occ", axis=0, tiled=True)
    padded = -(-rows // 8) * 8
    own = jnp.pad(own, ((0, padded - rows), (0, 0)))
    return add_mirror(mirror_row + padded, rows, [own, whole])


def solution(mesh):
    cores, chips = mesh.shape["occ"], mesh.shape["vir"]

    def body(*arrays):
        return shards(cores, chips, *arrays)

    return jax.shard_map(
        body,
        mesh=mesh,
        in_specs=(
            P("occ", "vir"),
            P("vir", "occ"),
            P(),
            P("occ", None),
            P(),
            P("occ", None),
            P("occ"),
        ),
        out_specs=P("occ", "vir"),
        check_vma=False,
    )
```

```python
import functools

import jax
import jax.numpy as jnp
from jax import lax
from jax.experimental import pallas as pl
from jax.experimental.pallas import tpu as pltpu
from jax.sharding import PartitionSpec as P


TILE = 128
SHARES = (384, 312, 240, 192)


LIMIT = 16 * 1024 * 1024
MIRROR_LIMIT = 24 * 1024 * 1024

SMEM = pl.BlockSpec(memory_space=pltpu.SMEM)
VMEM = pl.BlockSpec(memory_space=pltpu.VMEM)
ANY = pl.BlockSpec(memory_space=pl.ANY)


def row_chunks(rows, shares):
    edges = [0]
    for k in range(1, len(shares)):
        edges.append(rows * sum(shares[:k]) // sum(shares) // 8 * 8)
    edges.append(rows)
    return [(a, b - a) for a, b in zip(edges, edges[1:]) if b > a]


def other_core(a):
    return lax.ppermute(a, "occ", [(0, 1), (1, 0)])


def rows_kernel(chunks, a_ref, *refs):
    for (start, length), out in zip(chunks, refs):
        out[...] = a_ref[start : start + length, :]


def split_rows(a, chunks):
    return pl.pallas_call(
        functools.partial(rows_kernel, chunks),
        out_shape=[jax.ShapeDtypeStruct((length, a.shape[1]), a.dtype) for _, length in chunks],
        in_specs=[VMEM],
        out_specs=[VMEM] * len(chunks),
        compiler_params=pltpu.CompilerParams(vmem_limit_bytes=LIMIT),
        cost_estimate=pl.CostEstimate(flops=0, bytes_accessed=2 * a.size * 2, transcendentals=0),
        name="split_rows",
    )(a)


def sides_kernel(where_ref, map_hbm, v_hbm, send_ref, kept_ref, map_ref, v_ref, sems):
    side, first_row, first_col = where_ref[0], where_ref[1], where_ref[2]
    cols = v_ref.shape[0]
    tiles = cols // TILE
    map_copy = pltpu.make_async_copy(map_hbm, map_ref, sems.at[tiles])
    map_copy.start()

    def bands(r):
        band = pl.ds(r * TILE, TILE)
        return pltpu.make_async_copy(v_hbm.at[band], v_ref.at[band], sems.at[r])

    for r in range(tiles):
        bands(r).start()
    map_copy.wait()
    for r in range(tiles):
        bands(r).wait()
        for out, which in ((send_ref, 1 - side), (kept_ref, side)):
            for j in range(out.shape[1] // cols):
                block = 2 * j + which
                for c in range(tiles):
                    allowed = map_ref[first_row + r, first_col + block * tiles + c]
                    at = pl.multiple_of(block * cols + c * TILE, TILE)
                    tile = v_ref[r * TILE : (r + 1) * TILE, pl.ds(at, TILE)]
                    to = j * cols + c * TILE
                    out[r * TILE : (r + 1) * TILE, to : to + TILE] = jnp.where(
                        allowed == 1, tile, jnp.zeros_like(tile)
                    )


def split_sides(where, tile_map, integrals):
    cols, width = integrals.shape
    half = jax.ShapeDtypeStruct((cols, width // 2), integrals.dtype)
    return pl.pallas_call(
        sides_kernel,
        out_shape=[half, half],
        in_specs=[SMEM, ANY, ANY],
        out_specs=[VMEM, VMEM],
        scratch_shapes=[
            pltpu.SMEM(tile_map.shape, tile_map.dtype),
            pltpu.VMEM(integrals.shape, integrals.dtype),
            pltpu.SemaphoreType.DMA((cols // TILE + 1,)),
        ],
        compiler_params=pltpu.CompilerParams(vmem_limit_bytes=LIMIT),
        cost_estimate=pl.CostEstimate(
            flops=integrals.size, bytes_accessed=4 * integrals.size, transcendentals=0
        ),
        name="split_sides",
    )(where, tile_map, integrals)


def prepare_kernel(at_ref, *refs):
    *pieces, out_ref = refs
    cols = out_ref.shape[1]
    per_piece = pieces[0].shape[1] // cols
    for k in range(out_ref.shape[0] // cols):
        for p, piece in enumerate(pieces):
            at = at_ref[k] - p * per_piece

            @pl.when((at >= 0) & (at < per_piece))
            def _():
                block = piece[:, pl.ds(pl.multiple_of(at * cols, cols), cols)]
                out_ref[k * cols : (k + 1) * cols, :] = block.T


def prepare(at, pieces):
    cols = pieces[0].shape[0]
    depth = sum(piece.shape[1] for piece in pieces)
    return pl.pallas_call(
        prepare_kernel,
        out_shape=jax.ShapeDtypeStruct((depth, cols), pieces[0].dtype),
        in_specs=[SMEM] + [VMEM] * len(pieces),
        out_specs=VMEM,
        compiler_params=pltpu.CompilerParams(vmem_limit_bytes=LIMIT),
        cost_estimate=pl.CostEstimate(
            flops=0, bytes_accessed=4 * depth * cols, transcendentals=0
        ),
        name="prepare",
    )(at, *pieces)


def product_kernel(count, start, *refs):
    blocks = refs[:count]
    outs = len(refs[count:]) // 2
    integrals = refs[count : count + outs]
    base = None if start is None else refs[count + outs]
    row = jnp.concatenate([block[...] for block in blocks], axis=1)
    for k, out in enumerate(refs[-outs:]):
        result = jnp.dot(row, integrals[k][...], preferred_element_type=jnp.float32)
        if base is not None and k == outs - 1:
            result = result + base[start : start + out.shape[0], :]
        out[...] = result


def product(blocks, integrals, base=None, start=None):
    count = len(blocks)
    length, cols = blocks[0].shape
    given = [] if base is None else [base]
    return pl.pallas_call(
        functools.partial(product_kernel, count, start),
        out_shape=[jax.ShapeDtypeStruct((length, cols), jnp.float32)] * len(integrals),
        in_specs=[VMEM] * (count + len(integrals) + len(given)),
        out_specs=[VMEM] * len(integrals),
        compiler_params=pltpu.CompilerParams(vmem_limit_bytes=LIMIT),
        cost_estimate=pl.CostEstimate(
            flops=2 * len(integrals) * count * length * cols * cols,
            bytes_accessed=2 * count * (length + len(integrals) * cols) * cols,
            transcendentals=0,
        ),
        name="product",
    )(*blocks, *integrals, *given)


def for_groups(count, most, body):
    inline = max(u for u in range(1, most + 1) if count % u == 0)

    def step(i, carry):
        for u in range(inline):
            body(i * inline + u)
        return carry

    lax.fori_loop(0, count // inline, step, 0)


def mirror_kernel(offsets, own_count, index_ref, *refs):
    *pieces, out_ref, whole, picked = refs
    rows, cols = out_ref.shape
    lanes = cols // TILE

    for piece, offset in zip(pieces, offsets):

        def spread(g):
            at = pl.multiple_of(g * 8, 8)
            for c in range(lanes):
                whole[pl.ds(offset + at, 8), c, :] = piece[pl.ds(at, 8), c * TILE : (c + 1) * TILE]

        for_groups(piece.shape[0] // 8, 6, spread)

    def pick(g):
        for j in range(8):
            picked[g, :, j, :] = whole[index_ref[g * 8 + j]]

    for_groups(rows // 8, 6, pick)
    for j in range(rows % 8):
        picked[rows // 8, :, j, :] = whole[index_ref[rows // 8 * 8 + j]]

    odd = lax.broadcasted_iota(jnp.int32, (8, TILE), 1) % 2 == 1

    def finish(own, offset, g, size):
        at = g * 8 if isinstance(g, int) else pl.multiple_of(g * 8, 8)
        for c in range(lanes):
            part = picked[offset // 8 + g, c]
            swapped = jnp.where(odd, pltpu.roll(part, 1, 1), pltpu.roll(part, TILE - 1, 1))
            out_ref[pl.ds(offset + at, size), c * TILE : (c + 1) * TILE] = (
                own[pl.ds(at, size), c * TILE : (c + 1) * TILE] + swapped[:size]
            )

    for own, offset in zip(pieces[:own_count], offsets):
        length = min(own.shape[0], rows - offset)
        for_groups(length // 8, 48, functools.partial(finish, own, offset, size=8))
        if length % 8:
            finish(own, offset, length // 8, length % 8)


def add_mirror(index, rows, own, others):
    cols = own[0].shape[1]
    offsets, total = [], 0
    for piece in (*own, *others):
        offsets.append(total)
        total += piece.shape[0]
    return pl.pallas_call(
        functools.partial(mirror_kernel, tuple(offsets), len(own)),
        out_shape=jax.ShapeDtypeStruct((rows, cols), jnp.float32),
        in_specs=[SMEM] + [VMEM] * (len(own) + len(others)),
        out_specs=VMEM,
        scratch_shapes=[
            pltpu.VMEM((total, cols // TILE, TILE), jnp.float32),
            pltpu.VMEM((-(-rows // 8), cols // TILE, 8, TILE), jnp.float32),
        ],
        compiler_params=pltpu.CompilerParams(vmem_limit_bytes=MIRROR_LIMIT),
        cost_estimate=pl.CostEstimate(
            flops=rows * cols, bytes_accessed=(total + rows) * cols * 4, transcendentals=0
        ),
        name="mirror",
    )(index, *own, *others)


def shards(cores, chips, amplitudes, ladder_ints, tile_map, hole_ints, occ_energy, pair_list, mirror_row):
    rows, cols = amplitudes.shape
    integral_cols = ladder_ints.shape[1]
    vir_place = lax.axis_index("vir")
    occ_place = lax.axis_index("occ")
    members = chips // 2
    half_blocks = integral_cols // cols // 2
    side = vir_place % 2
    group = vir_place // 2
    across = [(v, v ^ 1) for v in range(chips)]

    evens = (members + 1) // 2
    order = [2 * p if p < evens else 2 * (members - p) - 1 for p in range(members)]
    forward, backward = [], []
    for s in range(2):
        for k in range(members):
            here, there = 2 * order[k] + s, 2 * order[(k + 1) % members] + s
            forward.append((here, there))
            backward.append((there, here))
    place = jnp.where(group % 2 == 0, group // 2, members - (group + 1) // 2)
    own_half = occ_place * half_blocks if cores == 2 else 0

    ring_steps = sorted([*range((members + 1) // 2), *range(-(members // 2), 0)], key=abs)

    def positions():
        p = (place - jnp.array(ring_steps, jnp.int32)) % members
        g = jnp.where(p < evens, 2 * p, 2 * (members - p) - 1)
        return (g - own_half) % members

    def whole_k(a):
        if cores == 2:
            return [a, other_core(a)]
        return [lax.all_gather(a, "occ", axis=1, tiled=True)]

    chunks = row_chunks(rows, SHARES)
    mine = split_rows(amplitudes, chunks)

    where = jnp.stack([side, vir_place * (cols // TILE), occ_place * (integral_cols // TILE)])
    send, kept = split_sides(where.astype(jnp.int32), tile_map, ladder_ints)
    near = lax.ppermute(send, "vir", across)
    at = positions().astype(jnp.int32)
    kept_all = prepare(at, whole_k(kept))
    near_all = prepare(at, whole_k(near))

    if cores == 2:
        both = jnp.zeros((2 * rows, cols), amplitudes.dtype)
        both = lax.dynamic_update_slice(both, amplitudes, (occ_place * rows, 0))
        both = lax.dynamic_update_slice(both, other_core(amplitudes), ((1 - occ_place) * rows, 0))
    else:
        both = lax.all_gather(amplitudes, "occ", axis=0, tiled=True)
    orbital_ids = jnp.arange(occ_energy.shape[0], dtype=jnp.int32)
    one_hot = (pair_list[:, :, None] == orbital_ids[None, None, :]).astype(jnp.float32)
    pair_energy = jnp.sum(one_hot * occ_energy[None, None, :], axis=(1, 2))
    base = jnp.dot(hole_ints, both, preferred_element_type=jnp.float32)
    base = base - pair_energy[:, None] * amplitudes.astype(jnp.float32)

    raws = []
    for index, (start, length) in enumerate(chunks):
        ups = members // 2 if index % 2 == 0 else (members - 1) // 2
        blocks = {0: mine[index]}
        for step in range(1, ups + 1):
            blocks[step] = lax.ppermute(blocks[step - 1], "vir", forward)
        for step in range(1, members - ups):
            blocks[-step] = lax.ppermute(blocks[1 - step], "vir", backward)
        arrived = [blocks[step] if step in blocks else blocks[step + members] for step in ring_steps]
        if index < len(chunks) - 1:
            for_near, rest = product(arrived, [near_all, kept_all], base, start)
        else:
            (for_near,) = product(arrived, [near_all])
            (rest,) = product(arrived, [kept_all], base, start)
        from_near = lax.ppermute(for_near, "vir", across)
        raws.append(rest + from_near)

    if cores == 2:
        others = [other_core(raw) for raw in raws]
        return add_mirror((mirror_row - occ_place * rows) % (2 * rows), rows, raws, others)
    own = jnp.concatenate(raws, axis=0)
    whole = lax.all_gather(own, "occ", axis=0, tiled=True)
    padded = -(-rows // 8) * 8
    own = jnp.pad(own, ((0, padded - rows), (0, 0)))
    return add_mirror(mirror_row + padded, rows, [own], [whole])


def solution(mesh):
    cores, chips = mesh.shape["occ"], mesh.shape["vir"]

    def body(*arrays):
        return shards(cores, chips, *arrays)

    return jax.shard_map(
        body,
        mesh=mesh,
        in_specs=(
            P("occ", "vir"),
            P("vir", "occ"),
            P(),
            P("occ", None),
            P(),
            P("occ", None),
            P("occ"),
        ),
        out_specs=P("occ", "vir"),
        check_vma=False,
    )
```

```python
import functools

import jax
import jax.numpy as jnp
from jax import lax
from jax.experimental import pallas as pl
from jax.experimental.pallas import tpu as pltpu
from jax.sharding import PartitionSpec as P


TILE = 128
SHARES = (360, 320, 256, 192)


LIMIT = 16 * 1024 * 1024
MIRROR_LIMIT = 24 * 1024 * 1024

SMEM = pl.BlockSpec(memory_space=pltpu.SMEM)
VMEM = pl.BlockSpec(memory_space=pltpu.VMEM)
HBM = pl.BlockSpec(memory_space=pltpu.HBM)


def row_chunks(rows, shares):
    edges = [0]
    for k in range(1, len(shares)):
        edges.append(rows * sum(shares[:k]) // sum(shares) // 8 * 8)
    edges.append(rows)
    return [(a, b - a) for a, b in zip(edges, edges[1:]) if b > a]


def other_core(a):
    return lax.ppermute(a, "occ", [(0, 1), (1, 0)])


def parts_kernel(chunks, side_ref, *refs):
    sources = refs[: 1 + bool(chunks)]
    *outs, sems = refs[len(sources) :]
    v_hbm, sent = sources[0], outs[0]
    cols = sent.shape[0]
    copies = []
    for k, ((start, length), out) in enumerate(zip(chunks, outs[1:])):
        copies.append(pltpu.make_async_copy(sources[1].at[pl.ds(start, length)], out, sems.at[k]))
    for j in range(sent.shape[1] // cols):
        at = pl.multiple_of((2 * j + side_ref[0]) * cols, TILE)
        copies.append(
            pltpu.make_async_copy(
                v_hbm.at[:, pl.ds(at, cols)],
                sent.at[:, pl.ds(j * cols, cols)],
                sems.at[len(chunks) + j],
            )
        )
    for copy in copies:
        copy.start()
    for copy in copies:
        copy.wait()


def parts(side, integrals, amplitudes=None, chunks=()):
    cols, width = integrals.shape
    shapes = [jax.ShapeDtypeStruct((cols, width // 2), integrals.dtype)]
    shapes += [jax.ShapeDtypeStruct((length, cols), integrals.dtype) for _, length in chunks]
    given = [amplitudes] if chunks else []
    return pl.pallas_call(
        functools.partial(parts_kernel, tuple(chunks)),
        out_shape=shapes,
        in_specs=[SMEM] + [HBM] * (1 + len(given)),
        out_specs=[VMEM] * len(shapes),
        scratch_shapes=[pltpu.SemaphoreType.DMA((len(chunks) + width // cols // 2,))],
        compiler_params=pltpu.CompilerParams(vmem_limit_bytes=None if chunks else LIMIT),
        cost_estimate=pl.CostEstimate(
            flops=0, bytes_accessed=4 * integrals.size, transcendentals=0
        ),
        name="parts",
    )(side, integrals, *given)


def prepare_kernel(cols, index_ref, map_hbm, *refs):
    *pieces, out_ref, map_ref, sem = refs
    copy = pltpu.make_async_copy(map_hbm, map_ref, sem)
    copy.start()
    copy.wait()
    count = out_ref.shape[0] // cols
    per_piece = pieces[0].shape[1] // cols
    first_row = index_ref[2 * count]
    for k in range(count):
        for p, piece in enumerate(pieces):
            at = index_ref[k] - p * per_piece

            @pl.when((at >= 0) & (at < per_piece))
            def _():
                for c in range(0, cols, TILE):
                    for r in range(0, out_ref.shape[1], TILE):
                        allowed = map_ref[first_row + r // TILE, index_ref[count + k] + c // TILE]
                        from_col = pl.multiple_of(at * cols + c, TILE)
                        tile = piece[r : r + TILE, pl.ds(from_col, TILE)]
                        tile = jnp.where(allowed == 1, tile, jnp.zeros_like(tile))
                        out_ref[k * cols + c : k * cols + c + TILE, r : r + TILE] = tile.T


def prepare(index, tile_map, pieces, cols):
    depth = sum(piece.shape[1] for piece in pieces)
    width = pieces[0].shape[0]
    return pl.pallas_call(
        functools.partial(prepare_kernel, cols),
        out_shape=jax.ShapeDtypeStruct((depth, width), pieces[0].dtype),
        in_specs=[SMEM, HBM] + [VMEM] * len(pieces),
        out_specs=VMEM,
        scratch_shapes=[pltpu.SMEM(tile_map.shape, tile_map.dtype), pltpu.SemaphoreType.DMA],
        compiler_params=pltpu.CompilerParams(vmem_limit_bytes=LIMIT),
        cost_estimate=pl.CostEstimate(
            flops=0, bytes_accessed=4 * depth * width, transcendentals=0
        ),
        name="prepare",
    )(index, tile_map, *pieces)


def product_kernel(count, start, *refs):
    integrals, out = refs[count], refs[-1]
    row = jnp.concatenate([block[...] for block in refs[:count]], axis=1)
    result = jnp.dot(row, integrals[...], preferred_element_type=jnp.float32)
    if start is not None:
        result = result + refs[count + 1][start : start + out.shape[0], :]
    out[...] = result


def product(blocks, integrals, base=None, start=None):
    length, _ = blocks[0].shape
    given = [] if base is None else [base]
    depth, width = integrals.shape
    return pl.pallas_call(
        functools.partial(product_kernel, len(blocks), start),
        out_shape=jax.ShapeDtypeStruct((length, width), jnp.float32),
        in_specs=[VMEM] * (len(blocks) + 1 + len(given)),
        out_specs=VMEM,
        compiler_params=pltpu.CompilerParams(vmem_limit_bytes=LIMIT),
        cost_estimate=pl.CostEstimate(
            flops=2 * length * depth * width,
            bytes_accessed=2 * depth * (length + width),
            transcendentals=0,
        ),
        name="product",
    )(*blocks, integrals, *given)


def for_groups(count, most, body):
    inline = max(u for u in range(1, most + 1) if count % u == 0)

    def step(i, carry):
        for u in range(inline):
            body(i * inline + u)
        return carry

    lax.fori_loop(0, count // inline, step, 0)


def mirror_kernel(offsets, own_count, index_ref, *refs):
    *pieces, out_ref, whole, picked = refs
    rows, cols = out_ref.shape
    lanes = cols // TILE

    for piece, offset in zip(pieces, offsets):

        def spread(g):
            at = pl.multiple_of(g * 8, 8)
            for c in range(lanes):
                whole[pl.ds(offset + at, 8), c, :] = piece[pl.ds(at, 8), c * TILE : (c + 1) * TILE]

        for_groups(piece.shape[0] // 8, 6, spread)

    def pick(g):
        for j in range(8):
            picked[g, :, j, :] = whole[index_ref[g * 8 + j]]

    for_groups(rows // 8, 6, pick)
    for j in range(rows % 8):
        picked[rows // 8, :, j, :] = whole[index_ref[rows // 8 * 8 + j]]

    odd = lax.broadcasted_iota(jnp.int32, (8, TILE), 1) % 2 == 1

    def finish(own, offset, g, size):
        at = g * 8 if isinstance(g, int) else pl.multiple_of(g * 8, 8)
        for c in range(lanes):
            part = picked[offset // 8 + g, c]
            swapped = jnp.where(odd, pltpu.roll(part, 1, 1), pltpu.roll(part, TILE - 1, 1))
            out_ref[pl.ds(offset + at, size), c * TILE : (c + 1) * TILE] = (
                own[pl.ds(at, size), c * TILE : (c + 1) * TILE] + swapped[:size]
            )

    for own, offset in zip(pieces[:own_count], offsets):
        length = min(own.shape[0], rows - offset)
        for_groups(length // 8, 48, functools.partial(finish, own, offset, size=8))
        if length % 8:
            finish(own, offset, length // 8, length % 8)


def add_mirror(index, rows, own, others):
    cols = own[0].shape[1]
    offsets, total = [], 0
    for piece in (*own, *others):
        offsets.append(total)
        total += piece.shape[0]
    return pl.pallas_call(
        functools.partial(mirror_kernel, tuple(offsets), len(own)),
        out_shape=jax.ShapeDtypeStruct((rows, cols), jnp.float32),
        in_specs=[SMEM] + [VMEM] * (len(own) + len(others)),
        out_specs=VMEM,
        scratch_shapes=[
            pltpu.VMEM((total, cols // TILE, TILE), jnp.float32),
            pltpu.VMEM((-(-rows // 8), cols // TILE, 8, TILE), jnp.float32),
        ],
        compiler_params=pltpu.CompilerParams(vmem_limit_bytes=MIRROR_LIMIT),
        cost_estimate=pl.CostEstimate(
            flops=rows * cols, bytes_accessed=(total + rows) * cols * 4, transcendentals=0
        ),
        name="mirror",
    )(index, *own, *others)


def spread_rows(piece, whole, offset):
    def spread(g):
        at = pl.multiple_of(g * 8, 8)
        for c in range(piece.shape[1] // TILE):
            whole[pl.ds(offset + at, 8), c, :] = piece[pl.ds(at, 8), c * TILE : (c + 1) * TILE]

    for_groups(piece.shape[0] // 8, 6, spread)


def early_kernel(index_ref, *refs):
    *pieces, picked, whole = refs
    offset = 0
    for piece in pieces:
        spread_rows(piece, whole, offset)
        offset += piece.shape[0]

    def pick(g):
        for j in range(8):
            picked[g * 8 + j] = whole[index_ref[g * 8 + j]]

    for_groups(index_ref.shape[0] // 8, 6, pick)


def late_kernel(target_ref, *refs):
    *own, other, _, out_hbm, picked, whole, out_ref, sems = refs
    spread_rows(own[-1], whole, 0)
    spread_rows(other, whole, other.shape[0])

    def put(g):
        for j in range(8):
            picked[target_ref[g * 8 + j]] = whole[g * 8 + j]

    for_groups(target_ref.shape[0] // 8, 6, put)

    odd = lax.broadcasted_iota(jnp.int32, (8, TILE), 1) % 2 == 1

    def finish(piece, offset, g):
        at = pl.multiple_of(g * 8, 8)
        for c in range(piece.shape[1] // TILE):
            part = picked[pl.ds(offset + at, 8), c, :]
            swapped = jnp.where(odd, pltpu.roll(part, 1, 1), pltpu.roll(part, TILE - 1, 1))
            out_ref[pl.ds(offset + at, 8), c * TILE : (c + 1) * TILE] = (
                piece[pl.ds(at, 8), c * TILE : (c + 1) * TILE] + swapped
            )

    offset = 0
    copies = []
    for k, piece in enumerate(own):
        for_groups(piece.shape[0] // 8, 48, functools.partial(finish, piece, offset))
        band = pl.ds(offset, piece.shape[0])
        copies.append(pltpu.make_async_copy(out_ref.at[band], out_hbm.at[band], sems.at[k]))
        copies[-1].start()
        offset += piece.shape[0]
    for copy in copies:
        copy.wait()


def add_mirror_in_steps(index, target, rows, own, others):
    cols = own[0].shape[1]
    early = [*own[:-1], *others[:-1]]
    slab = (cols // TILE, TILE)
    picked_shape = jax.ShapeDtypeStruct((rows + 8, *slab), jnp.float32)
    cost = pl.CostEstimate(flops=rows * cols, bytes_accessed=12 * rows * cols, transcendentals=0)
    params = pltpu.CompilerParams(vmem_limit_bytes=MIRROR_LIMIT)
    picked = pl.pallas_call(
        early_kernel,
        out_shape=picked_shape,
        in_specs=[SMEM] + [VMEM] * len(early),
        out_specs=VMEM,
        scratch_shapes=[pltpu.VMEM((sum(p.shape[0] for p in early), *slab), jnp.float32)],
        compiler_params=params,
        cost_estimate=cost,
        name="mirror_early",
    )(index, *early)
    return pl.pallas_call(
        late_kernel,
        out_shape=[jax.ShapeDtypeStruct((rows, cols), jnp.float32), picked_shape],
        in_specs=[SMEM] + [VMEM] * (len(own) + 2),
        out_specs=[HBM, VMEM],
        scratch_shapes=[
            pltpu.VMEM((2 * own[-1].shape[0], *slab), jnp.float32),
            pltpu.VMEM((rows, cols), jnp.float32),
            pltpu.SemaphoreType.DMA((len(own),)),
        ],
        input_output_aliases={len(own) + 2: 1},
        compiler_params=params,
        cost_estimate=cost,
        name="mirror_late",
    )(target, *own, others[-1], picked)[0]


def shards(cores, chips, amplitudes, ladder_ints, tile_map, hole_ints, occ_energy, pair_list, mirror_row):
    rows, cols = amplitudes.shape
    integral_cols = ladder_ints.shape[1]
    vir_place = lax.axis_index("vir")
    occ_place = lax.axis_index("occ")
    members = chips // 2
    half_blocks = integral_cols // cols // 2
    side = vir_place % 2
    group = vir_place // 2
    across = [(v, v ^ 1) for v in range(chips)]

    evens = (members + 1) // 2
    order = [2 * p if p < evens else 2 * (members - p) - 1 for p in range(members)]
    forward, backward = [], []
    for s in range(2):
        for k in range(members):
            here, there = 2 * order[k] + s, 2 * order[(k + 1) % members] + s
            forward.append((here, there))
            backward.append((there, here))
    place = jnp.where(group % 2 == 0, group // 2, members - (group + 1) // 2)
    own_half = occ_place * half_blocks if cores == 2 else 0

    ring_steps = sorted([*range((members + 1) // 2), *range(-(members // 2), 0)], key=abs)

    ring_place = (place - jnp.array(ring_steps, jnp.int32)) % members
    ring_group = jnp.where(ring_place < evens, 2 * ring_place, 2 * (members - ring_place) - 1)
    tiles = cols // TILE

    def tile_index(row_block):
        parts_of = [(ring_group - own_half) % members, (2 * ring_group + side) * tiles, row_block[None] * tiles]
        return jnp.concatenate([part.astype(jnp.int32) for part in parts_of])

    def whole_k(a):
        if cores == 2:
            return [a, other_core(a)]
        return [lax.all_gather(a, "occ", axis=1, tiled=True)]

    chunks = row_chunks(rows, SHARES)
    if rows % 8 == 0:
        send, *mine = parts((1 - side)[None].astype(jnp.int32), ladder_ints, amplitudes, chunks)
    else:
        (send,) = parts((1 - side)[None].astype(jnp.int32), ladder_ints)
        mine = [amplitudes[start : start + length] for start, length in chunks]
    near = lax.ppermute(send, "vir", across)
    (kept,) = parts(side[None].astype(jnp.int32), ladder_ints)
    kept_all = prepare(tile_index(vir_place), tile_map, whole_k(kept), cols)
    near_all = prepare(tile_index(vir_place + 1 - 2 * side), tile_map, whole_k(near), cols)

    if cores == 2:
        both = jnp.zeros((2 * rows, cols), amplitudes.dtype)
        both = lax.dynamic_update_slice(both, amplitudes, (occ_place * rows, 0))
        both = lax.dynamic_update_slice(both, other_core(amplitudes), ((1 - occ_place) * rows, 0))
    else:
        both = lax.all_gather(amplitudes, "occ", axis=0, tiled=True)
    orbital_ids = jnp.arange(occ_energy.shape[0], dtype=jnp.int32)
    one_hot = (pair_list[:, :, None] == orbital_ids[None, None, :]).astype(jnp.float32)
    pair_energy = jnp.sum(one_hot * occ_energy[None, None, :], axis=(1, 2))
    base = jnp.dot(hole_ints, both, preferred_element_type=jnp.float32)
    base = base - pair_energy[:, None] * amplitudes.astype(jnp.float32)

    raws = []
    for index, (start, length) in enumerate(chunks):
        ups = members // 2 if index % 2 == 0 else (members - 1) // 2
        blocks = {0: mine[index]}
        for step in range(1, ups + 1):
            blocks[step] = lax.ppermute(blocks[step - 1], "vir", forward)
        for step in range(1, members - ups):
            blocks[-step] = lax.ppermute(blocks[1 - step], "vir", backward)
        arrived = [blocks[step] if step in blocks else blocks[step + members] for step in ring_steps]
        for_near = product(arrived, near_all)
        from_near = lax.ppermute(for_near, "vir", across)
        rest = product(arrived, kept_all, base, start)
        raws.append(rest + from_near)

    if cores == 2:
        others = [other_core(raw) for raw in raws]
        index = (mirror_row - occ_place * rows) % (2 * rows)
        if rows % 8 or len(chunks) < 2:
            return add_mirror(index, rows, raws, others)
        ahead = chunks[-1][0]
        late = jnp.concatenate([mirror_row[ahead:], other_core(mirror_row)[ahead:]])
        late = late - occ_place * rows
        target = jnp.where((late >= 0) & (late < rows), late, rows)
        index = jnp.where(index < ahead, index, index - rows + ahead)
        index = jnp.where(index >= 2 * ahead, 0, jnp.maximum(index, 0))
        return add_mirror_in_steps(index, target, rows, raws, others)
    own = jnp.concatenate(raws, axis=0)
    whole = lax.all_gather(own, "occ", axis=0, tiled=True)
    padded = -(-rows // 8) * 8
    own = jnp.pad(own, ((0, padded - rows), (0, 0)))
    return add_mirror(mirror_row + padded, rows, [own], [whole])


def solution(mesh):
    cores, chips = mesh.shape["occ"], mesh.shape["vir"]

    def body(*arrays):
        return shards(cores, chips, *arrays)

    return jax.shard_map(
        body,
        mesh=mesh,
        in_specs=(
            P("occ", "vir"),
            P("vir", "occ"),
            P(),
            P("occ", None),
            P(),
            P("occ", None),
            P("occ"),
        ),
        out_specs=P("occ", "vir"),
        check_vma=False,
    )
```

```python
import functools

import jax
import jax.numpy as jnp
from jax import lax
from jax.experimental import pallas as pl
from jax.experimental.pallas import tpu as pltpu
from jax.sharding import PartitionSpec as P


TILE = 128
SHARES = (360, 320, 256, 192)


LIMIT = 16 * 1024 * 1024
MIRROR_LIMIT = 24 * 1024 * 1024

SMEM = pl.BlockSpec(memory_space=pltpu.SMEM)
VMEM = pl.BlockSpec(memory_space=pltpu.VMEM)
HBM = pl.BlockSpec(memory_space=pltpu.HBM)
ANY = pl.BlockSpec(memory_space=pl.ANY)


def row_chunks(rows, shares):
    edges = [0]
    for k in range(1, len(shares)):
        edges.append(rows * sum(shares[:k]) // sum(shares) // 8 * 8)
    edges.append(rows)
    return [(a, b - a) for a, b in zip(edges, edges[1:]) if b > a]


def other_core(a):
    return lax.ppermute(a, "occ", [(0, 1), (1, 0)])


def parts_kernel(chunks, side_ref, *refs):
    sources = refs[: 1 + bool(chunks)]
    *outs, sems = refs[len(sources) :]
    v_hbm, sent = sources[0], outs[0]
    cols = sent.shape[0]
    copies = []
    for k, ((start, length), out) in enumerate(zip(chunks, outs[1:])):
        copies.append(pltpu.make_async_copy(sources[1].at[pl.ds(start, length)], out, sems.at[k]))
    for j in range(sent.shape[1] // cols):
        at = pl.multiple_of((2 * j + side_ref[0]) * cols, TILE)
        copies.append(
            pltpu.make_async_copy(
                v_hbm.at[:, pl.ds(at, cols)],
                sent.at[:, pl.ds(j * cols, cols)],
                sems.at[len(chunks) + j],
            )
        )
    for copy in copies:
        copy.start()
    for copy in copies:
        copy.wait()


def parts(side, integrals, amplitudes=None, chunks=()):
    cols, width = integrals.shape
    shapes = [jax.ShapeDtypeStruct((cols, width // 2), integrals.dtype)]
    shapes += [jax.ShapeDtypeStruct((length, cols), integrals.dtype) for _, length in chunks]
    given = [amplitudes] if chunks else []
    return pl.pallas_call(
        functools.partial(parts_kernel, tuple(chunks)),
        out_shape=shapes,
        in_specs=[SMEM] + [HBM] * (1 + len(given)),
        out_specs=[VMEM] * len(shapes),
        scratch_shapes=[pltpu.SemaphoreType.DMA((len(chunks) + width // cols // 2,))],
        compiler_params=pltpu.CompilerParams(vmem_limit_bytes=None if chunks else LIMIT),
        cost_estimate=pl.CostEstimate(
            flops=0, bytes_accessed=4 * integrals.size, transcendentals=0
        ),
        name="parts",
    )(side, integrals, *given)


def prepare_kernel(cols, index_ref, map_hbm, *refs):
    *pieces, out_ref, map_ref, sem = refs
    copy = pltpu.make_async_copy(map_hbm, map_ref, sem)
    copy.start()
    copy.wait()
    count = out_ref.shape[0] // cols
    per_piece = pieces[0].shape[1] // cols
    first_row = index_ref[2 * count]
    for k in range(count):
        for p, piece in enumerate(pieces):
            at = index_ref[k] - p * per_piece

            @pl.when((at >= 0) & (at < per_piece))
            def _():
                for c in range(0, cols, TILE):
                    for r in range(0, out_ref.shape[1], TILE):
                        allowed = map_ref[first_row + r // TILE, index_ref[count + k] + c // TILE]
                        from_col = pl.multiple_of(at * cols + c, TILE)
                        tile = piece[r : r + TILE, pl.ds(from_col, TILE)]
                        tile = jnp.where(allowed == 1, tile, jnp.zeros_like(tile))
                        out_ref[k * cols + c : k * cols + c + TILE, r : r + TILE] = tile.T


def prepare(index, tile_map, pieces, cols):
    depth = sum(piece.shape[1] for piece in pieces)
    width = pieces[0].shape[0]
    return pl.pallas_call(
        functools.partial(prepare_kernel, cols),
        out_shape=jax.ShapeDtypeStruct((depth, width), pieces[0].dtype),
        in_specs=[SMEM, HBM] + [VMEM] * len(pieces),
        out_specs=VMEM,
        scratch_shapes=[pltpu.SMEM(tile_map.shape, tile_map.dtype), pltpu.SemaphoreType.DMA],
        compiler_params=pltpu.CompilerParams(vmem_limit_bytes=LIMIT),
        cost_estimate=pl.CostEstimate(
            flops=0, bytes_accessed=4 * depth * width, transcendentals=0
        ),
        name="prepare",
    )(index, tile_map, *pieces)


FETCHED = 2


def product_kernel(count, start, *refs):
    blocks, integrals = refs[:count], refs[count]
    out, fetched, sems = refs[-3:]
    near = count - FETCHED
    cols = out.shape[1]
    copies = [
        pltpu.make_async_copy(block, fetched.at[k], sems.at[k]) for k, block in enumerate(blocks[near:])
    ]
    for copy in copies:
        copy.start()
    row = jnp.concatenate([block[...] for block in blocks[:near]], axis=1)
    first = jnp.dot(row, integrals[: near * cols, :], preferred_element_type=jnp.float32)
    if start is not None:
        first = first + refs[count + 1][start : start + out.shape[0], :]
    out[...] = first
    for copy in copies:
        copy.wait()
    row = jnp.concatenate([fetched[k] for k in range(FETCHED)], axis=1)
    out[...] += jnp.dot(row, integrals[near * cols :, :], preferred_element_type=jnp.float32)


def product(blocks, integrals, base=None, start=None):
    length, cols = blocks[0].shape
    given = [] if base is None else [base]
    depth, width = integrals.shape
    return pl.pallas_call(
        functools.partial(product_kernel, len(blocks), start),
        out_shape=jax.ShapeDtypeStruct((length, width), jnp.float32),
        in_specs=[VMEM] * (len(blocks) - FETCHED) + [ANY] * FETCHED + [VMEM] * (1 + len(given)),
        out_specs=VMEM,
        scratch_shapes=[
            pltpu.VMEM((FETCHED, length, cols), blocks[0].dtype),
            pltpu.SemaphoreType.DMA((FETCHED,)),
        ],
        compiler_params=pltpu.CompilerParams(vmem_limit_bytes=LIMIT),
        cost_estimate=pl.CostEstimate(
            flops=2 * length * depth * width,
            bytes_accessed=2 * depth * (length + width),
            transcendentals=0,
        ),
        name="product",
    )(*blocks, integrals, *given)


def for_groups(count, most, body):
    inline = max(u for u in range(1, most + 1) if count % u == 0)

    def step(i, carry):
        for u in range(inline):
            body(i * inline + u)
        return carry

    lax.fori_loop(0, count // inline, step, 0)


def mirror_kernel(offsets, own_count, index_ref, *refs):
    *pieces, out_ref, whole, picked = refs
    rows, cols = out_ref.shape
    lanes = cols // TILE

    for piece, offset in zip(pieces, offsets):

        def spread(g):
            at = pl.multiple_of(g * 8, 8)
            for c in range(lanes):
                whole[pl.ds(offset + at, 8), c, :] = piece[pl.ds(at, 8), c * TILE : (c + 1) * TILE]

        for_groups(piece.shape[0] // 8, 6, spread)

    def pick(g):
        for j in range(8):
            picked[g, :, j, :] = whole[index_ref[g * 8 + j]]

    for_groups(rows // 8, 6, pick)
    for j in range(rows % 8):
        picked[rows // 8, :, j, :] = whole[index_ref[rows // 8 * 8 + j]]

    odd = lax.broadcasted_iota(jnp.int32, (8, TILE), 1) % 2 == 1

    def finish(own, offset, g, size):
        at = g * 8 if isinstance(g, int) else pl.multiple_of(g * 8, 8)
        for c in range(lanes):
            part = picked[offset // 8 + g, c]
            swapped = jnp.where(odd, pltpu.roll(part, 1, 1), pltpu.roll(part, TILE - 1, 1))
            out_ref[pl.ds(offset + at, size), c * TILE : (c + 1) * TILE] = (
                own[pl.ds(at, size), c * TILE : (c + 1) * TILE] + swapped[:size]
            )

    for own, offset in zip(pieces[:own_count], offsets):
        length = min(own.shape[0], rows - offset)
        for_groups(length // 8, 48, functools.partial(finish, own, offset, size=8))
        if length % 8:
            finish(own, offset, length // 8, length % 8)


def add_mirror(index, rows, own, others):
    cols = own[0].shape[1]
    offsets, total = [], 0
    for piece in (*own, *others):
        offsets.append(total)
        total += piece.shape[0]
    return pl.pallas_call(
        functools.partial(mirror_kernel, tuple(offsets), len(own)),
        out_shape=jax.ShapeDtypeStruct((rows, cols), jnp.float32),
        in_specs=[SMEM] + [VMEM] * (len(own) + len(others)),
        out_specs=VMEM,
        scratch_shapes=[
            pltpu.VMEM((total, cols // TILE, TILE), jnp.float32),
            pltpu.VMEM((-(-rows // 8), cols // TILE, 8, TILE), jnp.float32),
        ],
        compiler_params=pltpu.CompilerParams(vmem_limit_bytes=MIRROR_LIMIT),
        cost_estimate=pl.CostEstimate(
            flops=rows * cols, bytes_accessed=(total + rows) * cols * 4, transcendentals=0
        ),
        name="mirror",
    )(index, *own, *others)


def spread_rows(piece, whole, offset):
    def spread(g):
        at = pl.multiple_of(g * 8, 8)
        for c in range(piece.shape[1] // TILE):
            whole[pl.ds(offset + at, 8), c, :] = piece[pl.ds(at, 8), c * TILE : (c + 1) * TILE]

    for_groups(piece.shape[0] // 8, 6, spread)


def early_kernel(index_ref, *refs):
    *pieces, picked, whole = refs
    offset = 0
    for piece in pieces:
        spread_rows(piece, whole, offset)
        offset += piece.shape[0]

    def pick(g):
        for j in range(8):
            picked[g * 8 + j] = whole[index_ref[g * 8 + j]]

    for_groups(index_ref.shape[0] // 8, 6, pick)


def late_kernel(target_ref, *refs):
    *own, other, _, out_hbm, picked, whole, out_ref, sems = refs
    spread_rows(own[-1], whole, 0)
    spread_rows(other, whole, other.shape[0])

    def put(g):
        for j in range(8):
            picked[target_ref[g * 8 + j]] = whole[g * 8 + j]

    for_groups(target_ref.shape[0] // 8, 6, put)

    odd = lax.broadcasted_iota(jnp.int32, (8, TILE), 1) % 2 == 1

    def finish(piece, offset, g):
        at = pl.multiple_of(g * 8, 8)
        for c in range(piece.shape[1] // TILE):
            part = picked[pl.ds(offset + at, 8), c, :]
            swapped = jnp.where(odd, pltpu.roll(part, 1, 1), pltpu.roll(part, TILE - 1, 1))
            out_ref[pl.ds(offset + at, 8), c * TILE : (c + 1) * TILE] = (
                piece[pl.ds(at, 8), c * TILE : (c + 1) * TILE] + swapped
            )

    offset = 0
    copies = []
    for k, piece in enumerate(own):
        for_groups(piece.shape[0] // 8, 48, functools.partial(finish, piece, offset))
        band = pl.ds(offset, piece.shape[0])
        copies.append(pltpu.make_async_copy(out_ref.at[band], out_hbm.at[band], sems.at[k]))
        copies[-1].start()
        offset += piece.shape[0]
    for copy in copies:
        copy.wait()


def add_mirror_in_steps(index, target, rows, own, others):
    cols = own[0].shape[1]
    early = [*own[:-1], *others[:-1]]
    slab = (cols // TILE, TILE)
    picked_shape = jax.ShapeDtypeStruct((rows + 8, *slab), jnp.float32)
    cost = pl.CostEstimate(flops=rows * cols, bytes_accessed=12 * rows * cols, transcendentals=0)
    params = pltpu.CompilerParams(vmem_limit_bytes=MIRROR_LIMIT)
    picked = pl.pallas_call(
        early_kernel,
        out_shape=picked_shape,
        in_specs=[SMEM] + [VMEM] * len(early),
        out_specs=VMEM,
        scratch_shapes=[pltpu.VMEM((sum(p.shape[0] for p in early), *slab), jnp.float32)],
        compiler_params=params,
        cost_estimate=cost,
        name="mirror_early",
    )(index, *early)
    return pl.pallas_call(
        late_kernel,
        out_shape=[jax.ShapeDtypeStruct((rows, cols), jnp.float32), picked_shape],
        in_specs=[SMEM] + [VMEM] * (len(own) + 2),
        out_specs=[HBM, VMEM],
        scratch_shapes=[
            pltpu.VMEM((2 * own[-1].shape[0], *slab), jnp.float32),
            pltpu.VMEM((rows, cols), jnp.float32),
            pltpu.SemaphoreType.DMA((len(own),)),
        ],
        input_output_aliases={len(own) + 2: 1},
        compiler_params=params,
        cost_estimate=cost,
        name="mirror_late",
    )(target, *own, others[-1], picked)[0]


def shards(cores, chips, amplitudes, ladder_ints, tile_map, hole_ints, occ_energy, pair_list, mirror_row):
    rows, cols = amplitudes.shape
    integral_cols = ladder_ints.shape[1]
    vir_place = lax.axis_index("vir")
    occ_place = lax.axis_index("occ")
    members = chips // 2
    half_blocks = integral_cols // cols // 2
    side = vir_place % 2
    group = vir_place // 2
    across = [(v, v ^ 1) for v in range(chips)]

    evens = (members + 1) // 2
    order = [2 * p if p < evens else 2 * (members - p) - 1 for p in range(members)]
    forward, backward = [], []
    for s in range(2):
        for k in range(members):
            here, there = 2 * order[k] + s, 2 * order[(k + 1) % members] + s
            forward.append((here, there))
            backward.append((there, here))
    place = jnp.where(group % 2 == 0, group // 2, members - (group + 1) // 2)
    own_half = occ_place * half_blocks if cores == 2 else 0

    ring_steps = [*range((members + 1) // 2), *range(-(members // 2), 0)]
    ring_steps.sort(key=lambda step: (abs(step) == 1, abs(step)))

    ring_place = (place - jnp.array(ring_steps, jnp.int32)) % members
    ring_group = jnp.where(ring_place < evens, 2 * ring_place, 2 * (members - ring_place) - 1)
    tiles = cols // TILE

    def tile_index(row_block):
        parts_of = [(ring_group - own_half) % members, (2 * ring_group + side) * tiles, row_block[None] * tiles]
        return jnp.concatenate([part.astype(jnp.int32) for part in parts_of])

    def whole_k(a):
        if cores == 2:
            return [a, other_core(a)]
        return [lax.all_gather(a, "occ", axis=1, tiled=True)]

    chunks = row_chunks(rows, SHARES)
    if rows % 8 == 0:
        send, *mine = parts((1 - side)[None].astype(jnp.int32), ladder_ints, amplitudes, chunks)
    else:
        (send,) = parts((1 - side)[None].astype(jnp.int32), ladder_ints)
        mine = [amplitudes[start : start + length] for start, length in chunks]
    near = lax.ppermute(send, "vir", across)
    (kept,) = parts(side[None].astype(jnp.int32), ladder_ints)
    kept_all = prepare(tile_index(vir_place), tile_map, whole_k(kept), cols)
    near_all = prepare(tile_index(vir_place + 1 - 2 * side), tile_map, whole_k(near), cols)

    if cores == 2:
        both = jnp.zeros((2 * rows, cols), amplitudes.dtype)
        both = lax.dynamic_update_slice(both, amplitudes, (occ_place * rows, 0))
        both = lax.dynamic_update_slice(both, other_core(amplitudes), ((1 - occ_place) * rows, 0))
    else:
        both = lax.all_gather(amplitudes, "occ", axis=0, tiled=True)
    orbital_ids = jnp.arange(occ_energy.shape[0], dtype=jnp.int32)
    one_hot = (pair_list[:, :, None] == orbital_ids[None, None, :]).astype(jnp.float32)
    pair_energy = jnp.sum(one_hot * occ_energy[None, None, :], axis=(1, 2))
    base = jnp.dot(hole_ints, both, preferred_element_type=jnp.float32)
    base = base - pair_energy[:, None] * amplitudes.astype(jnp.float32)

    raws = []
    for index, (start, length) in enumerate(chunks):
        ups = members // 2 if index % 2 == 0 else (members - 1) // 2
        blocks = {0: mine[index]}
        for step in range(1, ups + 1):
            blocks[step] = lax.ppermute(blocks[step - 1], "vir", forward)
        for step in range(1, members - ups):
            blocks[-step] = lax.ppermute(blocks[1 - step], "vir", backward)
        arrived = [blocks[step] if step in blocks else blocks[step + members] for step in ring_steps]
        for_near = product(arrived, near_all)
        from_near = lax.ppermute(for_near, "vir", across)
        rest = product(arrived, kept_all, base, start)
        raws.append(rest + from_near)

    if cores == 2:
        others = [other_core(raw) for raw in raws]
        index = (mirror_row - occ_place * rows) % (2 * rows)
        if rows % 8 or len(chunks) < 2:
            return add_mirror(index, rows, raws, others)
        ahead = chunks[-1][0]
        late = jnp.concatenate([mirror_row[ahead:], other_core(mirror_row)[ahead:]])
        late = late - occ_place * rows
        target = jnp.where((late >= 0) & (late < rows), late, rows)
        index = jnp.where(index < ahead, index, index - rows + ahead)
        index = jnp.where(index >= 2 * ahead, 0, jnp.maximum(index, 0))
        return add_mirror_in_steps(index, target, rows, raws, others)
    own = jnp.concatenate(raws, axis=0)
    whole = lax.all_gather(own, "occ", axis=0, tiled=True)
    padded = -(-rows // 8) * 8
    own = jnp.pad(own, ((0, padded - rows), (0, 0)))
    return add_mirror(mirror_row + padded, rows, [own], [whole])


def solution(mesh):
    cores, chips = mesh.shape["occ"], mesh.shape["vir"]

    def body(*arrays):
        return shards(cores, chips, *arrays)

    return jax.shard_map(
        body,
        mesh=mesh,
        in_specs=(
            P("occ", "vir"),
            P("vir", "occ"),
            P(),
            P("occ", None),
            P(),
            P("occ", None),
            P("occ"),
        ),
        out_specs=P("occ", "vir"),
        check_vma=False,
    )
```

```python
import functools

import jax
import jax.numpy as jnp
from jax import lax
from jax.experimental import pallas as pl
from jax.experimental.pallas import tpu as pltpu
from jax.sharding import PartitionSpec as P


TILE = 128
SHARES = (360, 320, 256, 192)

FETCHED = {0: (0,), 1: (1, -1)}


LIMIT = 16 * 1024 * 1024
MIRROR_LIMIT = 24 * 1024 * 1024

SMEM = pl.BlockSpec(memory_space=pltpu.SMEM)
VMEM = pl.BlockSpec(memory_space=pltpu.VMEM)
HBM = pl.BlockSpec(memory_space=pltpu.HBM)
ANY = pl.BlockSpec(memory_space=pl.ANY)


def row_chunks(rows, shares):
    edges = [0]
    for k in range(1, len(shares)):
        edges.append(rows * sum(shares[:k]) // sum(shares) // 8 * 8)
    edges.append(rows)
    return [(a, b - a) for a, b in zip(edges, edges[1:]) if b > a]


def other_core(a):
    return lax.ppermute(a, "occ", [(0, 1), (1, 0)])


def parts_kernel(chunks, side_ref, *refs):
    sources = refs[: 1 + bool(chunks)]
    *outs, sems = refs[len(sources) :]
    v_hbm, sent = sources[0], outs[0]
    cols = sent.shape[0]
    copies = []
    for k, ((start, length), out) in enumerate(zip(chunks, outs[1:])):
        copies.append(pltpu.make_async_copy(sources[1].at[pl.ds(start, length)], out, sems.at[k]))
    for j in range(sent.shape[1] // cols):
        at = pl.multiple_of((2 * j + side_ref[0]) * cols, TILE)
        copies.append(
            pltpu.make_async_copy(
                v_hbm.at[:, pl.ds(at, cols)],
                sent.at[:, pl.ds(j * cols, cols)],
                sems.at[len(chunks) + j],
            )
        )
    for copy in copies:
        copy.start()
    for copy in copies:
        copy.wait()


def parts(side, integrals, amplitudes=None, chunks=()):
    cols, width = integrals.shape
    shapes = [jax.ShapeDtypeStruct((cols, width // 2), integrals.dtype)]
    shapes += [jax.ShapeDtypeStruct((length, cols), integrals.dtype) for _, length in chunks]
    given = [amplitudes] if chunks else []
    return pl.pallas_call(
        functools.partial(parts_kernel, tuple(chunks)),
        out_shape=shapes,
        in_specs=[SMEM] + [HBM] * (1 + len(given)),
        out_specs=[VMEM] * len(shapes),
        scratch_shapes=[pltpu.SemaphoreType.DMA((len(chunks) + width // cols // 2,))],
        compiler_params=pltpu.CompilerParams(vmem_limit_bytes=None if chunks else LIMIT),
        cost_estimate=pl.CostEstimate(
            flops=0, bytes_accessed=4 * integrals.size, transcendentals=0
        ),
        name="parts",
    )(side, integrals, *given)


def prepare_kernel(cols, index_ref, map_hbm, *refs):
    *pieces, out_ref, map_ref, sem = refs
    copy = pltpu.make_async_copy(map_hbm, map_ref, sem)
    copy.start()
    copy.wait()
    count = out_ref.shape[0] // cols
    per_piece = pieces[0].shape[1] // cols
    first_row = index_ref[2 * count]
    for k in range(count):
        for p, piece in enumerate(pieces):
            at = index_ref[k] - p * per_piece

            @pl.when((at >= 0) & (at < per_piece))
            def _():
                for c in range(0, cols, TILE):
                    for r in range(0, out_ref.shape[1], TILE):
                        allowed = map_ref[first_row + r // TILE, index_ref[count + k] + c // TILE]
                        from_col = pl.multiple_of(at * cols + c, TILE)
                        tile = piece[r : r + TILE, pl.ds(from_col, TILE)]
                        tile = jnp.where(allowed == 1, tile, jnp.zeros_like(tile))
                        out_ref[k * cols + c : k * cols + c + TILE, r : r + TILE] = tile.T


def prepare(index, tile_map, pieces, cols):
    depth = sum(piece.shape[1] for piece in pieces)
    width = pieces[0].shape[0]
    return pl.pallas_call(
        functools.partial(prepare_kernel, cols),
        out_shape=jax.ShapeDtypeStruct((depth, width), pieces[0].dtype),
        in_specs=[SMEM, HBM] + [VMEM] * len(pieces),
        out_specs=VMEM,
        scratch_shapes=[pltpu.SMEM(tile_map.shape, tile_map.dtype), pltpu.SemaphoreType.DMA],
        compiler_params=pltpu.CompilerParams(vmem_limit_bytes=LIMIT),
        cost_estimate=pl.CostEstimate(
            flops=0, bytes_accessed=4 * depth * width, transcendentals=0
        ),
        name="prepare",
    )(index, tile_map, *pieces)


def product_kernel(count, fetched, start, *refs):
    blocks, integrals = refs[:count], refs[count]
    out = refs[count + 1 + (start is not None)]
    cols = blocks[0].shape[1]

    def some(values, places):
        row = jnp.concatenate(values, axis=1)
        parts = [integrals[k * cols : (k + 1) * cols, :] for k in places]
        return jnp.dot(row, jnp.concatenate(parts, axis=0), preferred_element_type=jnp.float32)

    copies = []
    for n, k in enumerate(fetched):
        copies.append(pltpu.make_async_copy(blocks[k], refs[-2].at[n], refs[-1].at[n]))
        copies[-1].start()
    here = [k for k in range(count) if k not in fetched]
    first = some([blocks[k][...] for k in here], here)
    if start is not None:
        first = first + refs[count + 1][start : start + out.shape[0], :]
    out[...] = first
    if fetched:
        for copy in copies:
            copy.wait()
        out[...] += some([refs[-2][n] for n in range(len(fetched))], fetched)


def product(blocks, integrals, fetched=(), base=None, start=None):
    length, cols = blocks[0].shape
    given = [] if base is None else [base]
    depth, width = integrals.shape
    scratch = [
        pltpu.VMEM((len(fetched), length, cols), blocks[0].dtype),
        pltpu.SemaphoreType.DMA((len(fetched),)),
    ]
    return pl.pallas_call(
        functools.partial(product_kernel, len(blocks), fetched, start),
        out_shape=jax.ShapeDtypeStruct((length, width), jnp.float32),
        in_specs=[ANY if k in fetched else VMEM for k in range(len(blocks))] + [VMEM] * (1 + len(given)),
        out_specs=VMEM,
        scratch_shapes=scratch if fetched else [],
        compiler_params=pltpu.CompilerParams(vmem_limit_bytes=LIMIT),
        cost_estimate=pl.CostEstimate(
            flops=2 * length * depth * width,
            bytes_accessed=2 * depth * (length + width),
            transcendentals=0,
        ),
        name="product",
    )(*blocks, integrals, *given)


def for_groups(count, most, body):
    inline = max(u for u in range(1, most + 1) if count % u == 0)

    def step(i, carry):
        for u in range(inline):
            body(i * inline + u)
        return carry

    lax.fori_loop(0, count // inline, step, 0)


def mirror_kernel(offsets, own_count, index_ref, *refs):
    *pieces, out_ref, whole, picked = refs
    rows, cols = out_ref.shape
    lanes = cols // TILE

    for piece, offset in zip(pieces, offsets):

        def spread(g):
            at = pl.multiple_of(g * 8, 8)
            for c in range(lanes):
                whole[pl.ds(offset + at, 8), c, :] = piece[pl.ds(at, 8), c * TILE : (c + 1) * TILE]

        for_groups(piece.shape[0] // 8, 6, spread)

    def pick(g):
        for j in range(8):
            picked[g, :, j, :] = whole[index_ref[g * 8 + j]]

    for_groups(rows // 8, 6, pick)
    for j in range(rows % 8):
        picked[rows // 8, :, j, :] = whole[index_ref[rows // 8 * 8 + j]]

    odd = lax.broadcasted_iota(jnp.int32, (8, TILE), 1) % 2 == 1

    def finish(own, offset, g, size):
        at = g * 8 if isinstance(g, int) else pl.multiple_of(g * 8, 8)
        for c in range(lanes):
            part = picked[offset // 8 + g, c]
            swapped = jnp.where(odd, pltpu.roll(part, 1, 1), pltpu.roll(part, TILE - 1, 1))
            out_ref[pl.ds(offset + at, size), c * TILE : (c + 1) * TILE] = (
                own[pl.ds(at, size), c * TILE : (c + 1) * TILE] + swapped[:size]
            )

    for own, offset in zip(pieces[:own_count], offsets):
        length = min(own.shape[0], rows - offset)
        for_groups(length // 8, 48, functools.partial(finish, own, offset, size=8))
        if length % 8:
            finish(own, offset, length // 8, length % 8)


def add_mirror(index, rows, own, others):
    cols = own[0].shape[1]
    offsets, total = [], 0
    for piece in (*own, *others):
        offsets.append(total)
        total += piece.shape[0]
    return pl.pallas_call(
        functools.partial(mirror_kernel, tuple(offsets), len(own)),
        out_shape=jax.ShapeDtypeStruct((rows, cols), jnp.float32),
        in_specs=[SMEM] + [VMEM] * (len(own) + len(others)),
        out_specs=VMEM,
        scratch_shapes=[
            pltpu.VMEM((total, cols // TILE, TILE), jnp.float32),
            pltpu.VMEM((-(-rows // 8), cols // TILE, 8, TILE), jnp.float32),
        ],
        compiler_params=pltpu.CompilerParams(vmem_limit_bytes=MIRROR_LIMIT),
        cost_estimate=pl.CostEstimate(
            flops=rows * cols, bytes_accessed=(total + rows) * cols * 4, transcendentals=0
        ),
        name="mirror",
    )(index, *own, *others)


def spread_rows(piece, whole, offset):
    def spread(g):
        at = pl.multiple_of(g * 8, 8)
        for c in range(piece.shape[1] // TILE):
            whole[pl.ds(offset + at, 8), c, :] = piece[pl.ds(at, 8), c * TILE : (c + 1) * TILE]

    for_groups(piece.shape[0] // 8, 6, spread)


def early_kernel(index_ref, *refs):
    *pieces, picked, whole = refs
    offset = 0
    for piece in pieces:
        spread_rows(piece, whole, offset)
        offset += piece.shape[0]

    def pick(g):
        for j in range(8):
            picked[g * 8 + j] = whole[index_ref[g * 8 + j]]

    for_groups(index_ref.shape[0] // 8, 6, pick)


def late_kernel(target_ref, *refs):
    *own, other, _, out_hbm, picked, whole, out_ref, sems = refs
    spread_rows(own[-1], whole, 0)
    spread_rows(other, whole, other.shape[0])

    def put(g):
        for j in range(8):
            picked[target_ref[g * 8 + j]] = whole[g * 8 + j]

    for_groups(target_ref.shape[0] // 8, 6, put)

    odd = lax.broadcasted_iota(jnp.int32, (8, TILE), 1) % 2 == 1

    def finish(piece, offset, g):
        at = pl.multiple_of(g * 8, 8)
        for c in range(piece.shape[1] // TILE):
            part = picked[pl.ds(offset + at, 8), c, :]
            swapped = jnp.where(odd, pltpu.roll(part, 1, 1), pltpu.roll(part, TILE - 1, 1))
            out_ref[pl.ds(offset + at, 8), c * TILE : (c + 1) * TILE] = (
                piece[pl.ds(at, 8), c * TILE : (c + 1) * TILE] + swapped
            )

    offset = 0
    copies = []
    for k, piece in enumerate(own):
        for_groups(piece.shape[0] // 8, 48, functools.partial(finish, piece, offset))
        band = pl.ds(offset, piece.shape[0])
        copies.append(pltpu.make_async_copy(out_ref.at[band], out_hbm.at[band], sems.at[k]))
        copies[-1].start()
        offset += piece.shape[0]
    for copy in copies:
        copy.wait()


def add_mirror_in_steps(index, target, rows, own, others):
    cols = own[0].shape[1]
    early = [*own[:-1], *others[:-1]]
    slab = (cols // TILE, TILE)
    picked_shape = jax.ShapeDtypeStruct((rows + 8, *slab), jnp.float32)
    cost = pl.CostEstimate(flops=rows * cols, bytes_accessed=12 * rows * cols, transcendentals=0)
    params = pltpu.CompilerParams(vmem_limit_bytes=MIRROR_LIMIT)
    picked = pl.pallas_call(
        early_kernel,
        out_shape=picked_shape,
        in_specs=[SMEM] + [VMEM] * len(early),
        out_specs=VMEM,
        scratch_shapes=[pltpu.VMEM((sum(p.shape[0] for p in early), *slab), jnp.float32)],
        compiler_params=params,
        cost_estimate=cost,
        name="mirror_early",
    )(index, *early)
    return pl.pallas_call(
        late_kernel,
        out_shape=[jax.ShapeDtypeStruct((rows, cols), jnp.float32), picked_shape],
        in_specs=[SMEM] + [VMEM] * (len(own) + 2),
        out_specs=[HBM, VMEM],
        scratch_shapes=[
            pltpu.VMEM((2 * own[-1].shape[0], *slab), jnp.float32),
            pltpu.VMEM((rows, cols), jnp.float32),
            pltpu.SemaphoreType.DMA((len(own),)),
        ],
        input_output_aliases={len(own) + 2: 1},
        compiler_params=params,
        cost_estimate=cost,
        name="mirror_late",
    )(target, *own, others[-1], picked)[0]


def shards(cores, chips, amplitudes, ladder_ints, tile_map, hole_ints, occ_energy, pair_list, mirror_row):
    rows, cols = amplitudes.shape
    integral_cols = ladder_ints.shape[1]
    vir_place = lax.axis_index("vir")
    occ_place = lax.axis_index("occ")
    members = chips // 2
    half_blocks = integral_cols // cols // 2
    side = vir_place % 2
    group = vir_place // 2
    across = [(v, v ^ 1) for v in range(chips)]

    evens = (members + 1) // 2
    order = [2 * p if p < evens else 2 * (members - p) - 1 for p in range(members)]
    forward, backward = [], []
    for s in range(2):
        for k in range(members):
            here, there = 2 * order[k] + s, 2 * order[(k + 1) % members] + s
            forward.append((here, there))
            backward.append((there, here))
    place = jnp.where(group % 2 == 0, group // 2, members - (group + 1) // 2)
    own_half = occ_place * half_blocks if cores == 2 else 0

    ring_steps = [*range((members + 1) // 2), *range(-(members // 2), 0)]
    ring_steps.sort(key=lambda step: (abs(step) == 1, abs(step)))

    ring_place = (place - jnp.array(ring_steps, jnp.int32)) % members
    ring_group = jnp.where(ring_place < evens, 2 * ring_place, 2 * (members - ring_place) - 1)
    tiles = cols // TILE

    def tile_index(row_block):
        parts_of = [(ring_group - own_half) % members, (2 * ring_group + side) * tiles, row_block[None] * tiles]
        return jnp.concatenate([part.astype(jnp.int32) for part in parts_of])

    def whole_k(a):
        if cores == 2:
            return [a, other_core(a)]
        return [lax.all_gather(a, "occ", axis=1, tiled=True)]

    chunks = row_chunks(rows, SHARES)
    if rows % 8 == 0:
        send, *mine = parts((1 - side)[None].astype(jnp.int32), ladder_ints, amplitudes, chunks)
    else:
        (send,) = parts((1 - side)[None].astype(jnp.int32), ladder_ints)
        mine = [amplitudes[start : start + length] for start, length in chunks]
    near = lax.ppermute(send, "vir", across)
    (kept,) = parts(side[None].astype(jnp.int32), ladder_ints)
    kept_all = prepare(tile_index(vir_place), tile_map, whole_k(kept), cols)
    near_all = prepare(tile_index(vir_place + 1 - 2 * side), tile_map, whole_k(near), cols)

    if cores == 2:
        both = jnp.zeros((2 * rows, cols), amplitudes.dtype)
        both = lax.dynamic_update_slice(both, amplitudes, (occ_place * rows, 0))
        both = lax.dynamic_update_slice(both, other_core(amplitudes), ((1 - occ_place) * rows, 0))
    else:
        both = lax.all_gather(amplitudes, "occ", axis=0, tiled=True)
    orbital_ids = jnp.arange(occ_energy.shape[0], dtype=jnp.int32)
    one_hot = (pair_list[:, :, None] == orbital_ids[None, None, :]).astype(jnp.float32)
    pair_energy = jnp.sum(one_hot * occ_energy[None, None, :], axis=(1, 2))
    base = jnp.dot(hole_ints, both, preferred_element_type=jnp.float32)
    base = base - pair_energy[:, None] * amplitudes.astype(jnp.float32)

    raws = []
    for index, (start, length) in enumerate(chunks):
        ups = members // 2 if index % 2 == 0 else (members - 1) // 2
        blocks = {0: mine[index]}
        for step in range(1, ups + 1):
            blocks[step] = lax.ppermute(blocks[step - 1], "vir", forward)
        for step in range(1, members - ups):
            blocks[-step] = lax.ppermute(blocks[1 - step], "vir", backward)
        arrived = [blocks[step] if step in blocks else blocks[step + members] for step in ring_steps]
        fetched = tuple(k for k, step in enumerate(ring_steps) if step in FETCHED.get(index, ()))
        for_near = product(arrived, near_all, fetched)
        from_near = lax.ppermute(for_near, "vir", across)
        rest = product(arrived, kept_all, fetched, base, start)
        raws.append(rest + from_near)

    if cores == 2:
        others = [other_core(raw) for raw in raws]
        index = (mirror_row - occ_place * rows) % (2 * rows)
        if rows % 8 or len(chunks) < 2:
            return add_mirror(index, rows, raws, others)
        ahead = chunks[-1][0]
        late = jnp.concatenate([mirror_row[ahead:], other_core(mirror_row)[ahead:]])
        late = late - occ_place * rows
        target = jnp.where((late >= 0) & (late < rows), late, rows)
        index = jnp.where(index < ahead, index, index - rows + ahead)
        index = jnp.where(index >= 2 * ahead, 0, jnp.maximum(index, 0))
        return add_mirror_in_steps(index, target, rows, raws, others)
    own = jnp.concatenate(raws, axis=0)
    whole = lax.all_gather(own, "occ", axis=0, tiled=True)
    padded = -(-rows // 8) * 8
    own = jnp.pad(own, ((0, padded - rows), (0, 0)))
    return add_mirror(mirror_row + padded, rows, [own], [whole])


def solution(mesh):
    cores, chips = mesh.shape["occ"], mesh.shape["vir"]

    def body(*arrays):
        return shards(cores, chips, *arrays)

    return jax.shard_map(
        body,
        mesh=mesh,
        in_specs=(
            P("occ", "vir"),
            P("vir", "occ"),
            P(),
            P("occ", None),
            P(),
            P("occ", None),
            P("occ"),
        ),
        out_specs=P("occ", "vir"),
        check_vma=False,
    )
```

```python
import functools

import jax
import jax.numpy as jnp
from jax import lax
from jax.experimental import pallas as pl
from jax.experimental.pallas import tpu as pltpu
from jax.sharding import PartitionSpec as P


TILE = 128
SHARES = (360, 320, 256, 192)

FETCHED = {0: (0,), 1: (1, -1)}


LIMIT = 16 * 1024 * 1024
MIRROR_LIMIT = 24 * 1024 * 1024

SMEM = pl.BlockSpec(memory_space=pltpu.SMEM)
VMEM = pl.BlockSpec(memory_space=pltpu.VMEM)
HBM = pl.BlockSpec(memory_space=pltpu.HBM)
ANY = pl.BlockSpec(memory_space=pl.ANY)


def row_chunks(rows, shares):
    edges = [0]
    for k in range(1, len(shares)):
        edges.append(rows * sum(shares[:k]) // sum(shares) // 8 * 8)
    edges.append(rows)
    return [(a, b - a) for a, b in zip(edges, edges[1:]) if b > a]


def other_core(a):
    return lax.ppermute(a, "occ", [(0, 1), (1, 0)])


def parts_kernel(chunks, side_ref, *refs):
    sources = refs[: 1 + bool(chunks)]
    *outs, sems = refs[len(sources) :]
    v_hbm, sent = sources[0], outs[0]
    cols = sent.shape[0]
    copies = []
    for k, ((start, length), out) in enumerate(zip(chunks, outs[1:])):
        copies.append(pltpu.make_async_copy(sources[1].at[pl.ds(start, length)], out, sems.at[k]))
    for j in range(sent.shape[1] // cols):
        at = pl.multiple_of((2 * j + side_ref[0]) * cols, TILE)
        copies.append(
            pltpu.make_async_copy(
                v_hbm.at[:, pl.ds(at, cols)],
                sent.at[:, pl.ds(j * cols, cols)],
                sems.at[len(chunks) + j],
            )
        )
    for copy in copies:
        copy.start()
    for copy in copies:
        copy.wait()


def parts(side, integrals, amplitudes=None, chunks=()):
    cols, width = integrals.shape
    shapes = [jax.ShapeDtypeStruct((cols, width // 2), integrals.dtype)]
    shapes += [jax.ShapeDtypeStruct((length, cols), integrals.dtype) for _, length in chunks]
    given = [amplitudes] if chunks else []
    return pl.pallas_call(
        functools.partial(parts_kernel, tuple(chunks)),
        out_shape=shapes,
        in_specs=[SMEM] + [HBM] * (1 + len(given)),
        out_specs=[VMEM] * len(shapes),
        scratch_shapes=[pltpu.SemaphoreType.DMA((len(chunks) + width // cols // 2,))],
        compiler_params=pltpu.CompilerParams(vmem_limit_bytes=None if chunks else LIMIT),
        cost_estimate=pl.CostEstimate(
            flops=0, bytes_accessed=4 * integrals.size, transcendentals=0
        ),
        name="parts",
    )(side, integrals, *given)


def prepare_kernel(cols, index_ref, map_hbm, *refs):
    *pieces, out_ref, map_ref, sem = refs
    copy = pltpu.make_async_copy(map_hbm, map_ref, sem)
    copy.start()
    copy.wait()
    count = out_ref.shape[0] // cols
    per_piece = pieces[0].shape[1] // cols
    first_row = index_ref[2 * count]
    for k in range(count):
        for p, piece in enumerate(pieces):
            at = index_ref[k] - p * per_piece

            @pl.when((at >= 0) & (at < per_piece))
            def _():
                for c in range(0, cols, TILE):
                    for r in range(0, out_ref.shape[1], TILE):
                        allowed = map_ref[first_row + r // TILE, index_ref[count + k] + c // TILE]
                        from_col = pl.multiple_of(at * cols + c, TILE)
                        tile = piece[r : r + TILE, pl.ds(from_col, TILE)]
                        tile = jnp.where(allowed == 1, tile, jnp.zeros_like(tile))
                        out_ref[k * cols + c : k * cols + c + TILE, r : r + TILE] = tile.T


def prepare(index, tile_map, pieces, cols):
    depth = sum(piece.shape[1] for piece in pieces)
    width = pieces[0].shape[0]
    return pl.pallas_call(
        functools.partial(prepare_kernel, cols),
        out_shape=jax.ShapeDtypeStruct((depth, width), pieces[0].dtype),
        in_specs=[SMEM, HBM] + [VMEM] * len(pieces),
        out_specs=VMEM,
        scratch_shapes=[pltpu.SMEM(tile_map.shape, tile_map.dtype), pltpu.SemaphoreType.DMA],
        compiler_params=pltpu.CompilerParams(vmem_limit_bytes=LIMIT),
        cost_estimate=pl.CostEstimate(
            flops=0, bytes_accessed=4 * depth * width, transcendentals=0
        ),
        name="prepare",
    )(index, tile_map, *pieces)


def product_kernel(count, fetched, start, *refs):
    blocks, integrals = refs[:count], refs[count]
    out = refs[count + 1 + (start is not None)]
    cols = blocks[0].shape[1]

    def some(values, places):
        row = jnp.concatenate(values, axis=1)
        parts = [integrals[k * cols : (k + 1) * cols, :] for k in places]
        return jnp.dot(row, jnp.concatenate(parts, axis=0), preferred_element_type=jnp.float32)

    copies = []
    for n, k in enumerate(fetched):
        copies.append(pltpu.make_async_copy(blocks[k], refs[-2].at[n], refs[-1].at[n]))
        copies[-1].start()
    here = [k for k in range(count) if k not in fetched]
    first = some([blocks[k][...] for k in here], here)
    if start is not None:
        first = first + refs[count + 1][start : start + out.shape[0], :]
    out[...] = first
    if fetched:
        for copy in copies:
            copy.wait()
        out[...] += some([refs[-2][n] for n in range(len(fetched))], fetched)


def product(blocks, integrals, fetched=(), base=None, start=None):
    length, cols = blocks[0].shape
    given = [] if base is None else [base]
    depth, width = integrals.shape
    scratch = [
        pltpu.VMEM((len(fetched), length, cols), blocks[0].dtype),
        pltpu.SemaphoreType.DMA((len(fetched),)),
    ]
    return pl.pallas_call(
        functools.partial(product_kernel, len(blocks), fetched, start),
        out_shape=jax.ShapeDtypeStruct((length, width), jnp.float32),
        in_specs=[ANY if k in fetched else VMEM for k in range(len(blocks))] + [VMEM] * (1 + len(given)),
        out_specs=VMEM,
        scratch_shapes=scratch if fetched else [],
        compiler_params=pltpu.CompilerParams(vmem_limit_bytes=LIMIT),
        cost_estimate=pl.CostEstimate(
            flops=2 * length * depth * width,
            bytes_accessed=2 * depth * (length + width),
            transcendentals=0,
        ),
        name="product",
    )(*blocks, integrals, *given)


def for_groups(count, most, body):
    inline = max(u for u in range(1, most + 1) if count % u == 0)

    def step(i, carry):
        for u in range(inline):
            body(i * inline + u)
        return carry

    lax.fori_loop(0, count // inline, step, 0)


def mirror_kernel(offsets, own_count, index_ref, *refs):
    *pieces, out_ref, whole, picked = refs
    rows, cols = out_ref.shape
    lanes = cols // TILE

    for piece, offset in zip(pieces, offsets):

        def spread(g):
            at = pl.multiple_of(g * 8, 8)
            for c in range(lanes):
                whole[pl.ds(offset + at, 8), c, :] = piece[pl.ds(at, 8), c * TILE : (c + 1) * TILE]

        for_groups(piece.shape[0] // 8, 6, spread)

    def pick(g):
        for j in range(8):
            picked[g, :, j, :] = whole[index_ref[g * 8 + j]]

    for_groups(rows // 8, 6, pick)
    for j in range(rows % 8):
        picked[rows // 8, :, j, :] = whole[index_ref[rows // 8 * 8 + j]]

    odd = lax.broadcasted_iota(jnp.int32, (8, TILE), 1) % 2 == 1

    def finish(own, offset, g, size):
        at = g * 8 if isinstance(g, int) else pl.multiple_of(g * 8, 8)
        for c in range(lanes):
            part = picked[offset // 8 + g, c]
            swapped = jnp.where(odd, pltpu.roll(part, 1, 1), pltpu.roll(part, TILE - 1, 1))
            out_ref[pl.ds(offset + at, size), c * TILE : (c + 1) * TILE] = (
                own[pl.ds(at, size), c * TILE : (c + 1) * TILE] + swapped[:size]
            )

    for own, offset in zip(pieces[:own_count], offsets):
        length = min(own.shape[0], rows - offset)
        for_groups(length // 8, 48, functools.partial(finish, own, offset, size=8))
        if length % 8:
            finish(own, offset, length // 8, length % 8)


def add_mirror(index, rows, own, others):
    cols = own[0].shape[1]
    offsets, total = [], 0
    for piece in (*own, *others):
        offsets.append(total)
        total += piece.shape[0]
    return pl.pallas_call(
        functools.partial(mirror_kernel, tuple(offsets), len(own)),
        out_shape=jax.ShapeDtypeStruct((rows, cols), jnp.float32),
        in_specs=[SMEM] + [VMEM] * (len(own) + len(others)),
        out_specs=VMEM,
        scratch_shapes=[
            pltpu.VMEM((total, cols // TILE, TILE), jnp.float32),
            pltpu.VMEM((-(-rows // 8), cols // TILE, 8, TILE), jnp.float32),
        ],
        compiler_params=pltpu.CompilerParams(vmem_limit_bytes=MIRROR_LIMIT),
        cost_estimate=pl.CostEstimate(
            flops=rows * cols, bytes_accessed=(total + rows) * cols * 4, transcendentals=0
        ),
        name="mirror",
    )(index, *own, *others)


def spread_rows(piece, whole, offset):
    def spread(g):
        at = pl.multiple_of(g * 8, 8)
        for c in range(piece.shape[1] // TILE):
            whole[pl.ds(offset + at, 8), c, :] = piece[pl.ds(at, 8), c * TILE : (c + 1) * TILE]

    for_groups(piece.shape[0] // 8, 24, spread)


def early_kernel(index_ref, *refs):
    *pieces, picked, whole = refs
    offset = 0
    for piece in pieces:
        spread_rows(piece, whole, offset)
        offset += piece.shape[0]

    def pick(g):
        for j in range(8):
            picked[g * 8 + j] = whole[index_ref[g * 8 + j]]

    for_groups(index_ref.shape[0] // 8, 48, pick)


def late_kernel(target_ref, *refs):
    *own, other, _, out_hbm, picked, whole, out_ref, sems = refs
    spread_rows(own[-1], whole, 0)
    spread_rows(other, whole, other.shape[0])

    def put(g):
        for j in range(8):
            picked[target_ref[g * 8 + j]] = whole[g * 8 + j]

    for_groups(target_ref.shape[0] // 8, 24, put)

    odd = lax.broadcasted_iota(jnp.int32, (8, TILE), 1) % 2 == 1

    def finish(piece, offset, g):
        at = pl.multiple_of(g * 8, 8)
        for c in range(piece.shape[1] // TILE):
            part = picked[pl.ds(offset + at, 8), c, :]
            swapped = jnp.where(odd, pltpu.roll(part, 1, 1), pltpu.roll(part, TILE - 1, 1))
            out_ref[pl.ds(offset + at, 8), c * TILE : (c + 1) * TILE] = (
                piece[pl.ds(at, 8), c * TILE : (c + 1) * TILE] + swapped
            )

    offset = 0
    copies = []
    for k, piece in enumerate(own):
        for_groups(piece.shape[0] // 8, 48, functools.partial(finish, piece, offset))
        band = pl.ds(offset, piece.shape[0])
        copies.append(pltpu.make_async_copy(out_ref.at[band], out_hbm.at[band], sems.at[k]))
        copies[-1].start()
        offset += piece.shape[0]
    for copy in copies:
        copy.wait()


def add_mirror_in_steps(index, target, rows, own, others):
    cols = own[0].shape[1]
    early = [*own[:-1], *others[:-1]]
    slab = (cols // TILE, TILE)
    picked_shape = jax.ShapeDtypeStruct((rows + 8, *slab), jnp.float32)
    cost = pl.CostEstimate(flops=rows * cols, bytes_accessed=12 * rows * cols, transcendentals=0)
    params = pltpu.CompilerParams(vmem_limit_bytes=MIRROR_LIMIT)
    picked = pl.pallas_call(
        early_kernel,
        out_shape=picked_shape,
        in_specs=[SMEM] + [VMEM] * len(early),
        out_specs=VMEM,
        scratch_shapes=[pltpu.VMEM((sum(p.shape[0] for p in early), *slab), jnp.float32)],
        compiler_params=params,
        cost_estimate=cost,
        name="mirror_early",
    )(index, *early)
    return pl.pallas_call(
        late_kernel,
        out_shape=[jax.ShapeDtypeStruct((rows, cols), jnp.float32), picked_shape],
        in_specs=[SMEM] + [VMEM] * (len(own) + 2),
        out_specs=[HBM, VMEM],
        scratch_shapes=[
            pltpu.VMEM((2 * own[-1].shape[0], *slab), jnp.float32),
            pltpu.VMEM((rows, cols), jnp.float32),
            pltpu.SemaphoreType.DMA((len(own),)),
        ],
        input_output_aliases={len(own) + 2: 1},
        compiler_params=params,
        cost_estimate=cost,
        name="mirror_late",
    )(target, *own, others[-1], picked)[0]


def shards(cores, chips, amplitudes, ladder_ints, tile_map, hole_ints, occ_energy, pair_list, mirror_row):
    rows, cols = amplitudes.shape
    integral_cols = ladder_ints.shape[1]
    vir_place = lax.axis_index("vir")
    occ_place = lax.axis_index("occ")
    members = chips // 2
    half_blocks = integral_cols // cols // 2
    side = vir_place % 2
    group = vir_place // 2
    across = [(v, v ^ 1) for v in range(chips)]

    evens = (members + 1) // 2
    order = [2 * p if p < evens else 2 * (members - p) - 1 for p in range(members)]
    forward, backward = [], []
    for s in range(2):
        for k in range(members):
            here, there = 2 * order[k] + s, 2 * order[(k + 1) % members] + s
            forward.append((here, there))
            backward.append((there, here))
    place = jnp.where(group % 2 == 0, group // 2, members - (group + 1) // 2)
    own_half = occ_place * half_blocks if cores == 2 else 0

    ring_steps = [*range((members + 1) // 2), *range(-(members // 2), 0)]
    ring_steps.sort(key=lambda step: (abs(step) == 1, abs(step)))

    ring_place = (place - jnp.array(ring_steps, jnp.int32)) % members
    ring_group = jnp.where(ring_place < evens, 2 * ring_place, 2 * (members - ring_place) - 1)
    tiles = cols // TILE

    def tile_index(row_block):
        parts_of = [(ring_group - own_half) % members, (2 * ring_group + side) * tiles, row_block[None] * tiles]
        return jnp.concatenate([part.astype(jnp.int32) for part in parts_of])

    def whole_k(a):
        if cores == 2:
            return [a, other_core(a)]
        return [lax.all_gather(a, "occ", axis=1, tiled=True)]

    chunks = row_chunks(rows, SHARES)
    if rows % 8 == 0:
        send, *mine = parts((1 - side)[None].astype(jnp.int32), ladder_ints, amplitudes, chunks)
    else:
        (send,) = parts((1 - side)[None].astype(jnp.int32), ladder_ints)
        mine = [amplitudes[start : start + length] for start, length in chunks]
    near = lax.ppermute(send, "vir", across)
    (kept,) = parts(side[None].astype(jnp.int32), ladder_ints)
    kept_all = prepare(tile_index(vir_place), tile_map, whole_k(kept), cols)
    near_all = prepare(tile_index(vir_place + 1 - 2 * side), tile_map, whole_k(near), cols)

    if cores == 2:
        both = jnp.zeros((2 * rows, cols), amplitudes.dtype)
        both = lax.dynamic_update_slice(both, amplitudes, (occ_place * rows, 0))
        both = lax.dynamic_update_slice(both, other_core(amplitudes), ((1 - occ_place) * rows, 0))
    else:
        both = lax.all_gather(amplitudes, "occ", axis=0, tiled=True)
    orbital_ids = jnp.arange(occ_energy.shape[0], dtype=jnp.int32)
    one_hot = (pair_list[:, :, None] == orbital_ids[None, None, :]).astype(jnp.float32)
    pair_energy = jnp.sum(one_hot * occ_energy[None, None, :], axis=(1, 2))
    base = jnp.dot(hole_ints, both, preferred_element_type=jnp.float32)
    base = base - pair_energy[:, None] * amplitudes.astype(jnp.float32)

    raws = []
    for index, (start, length) in enumerate(chunks):
        ups = members // 2 if index % 2 == 0 else (members - 1) // 2
        blocks = {0: mine[index]}
        for step in range(1, ups + 1):
            blocks[step] = lax.ppermute(blocks[step - 1], "vir", forward)
        for step in range(1, members - ups):
            blocks[-step] = lax.ppermute(blocks[1 - step], "vir", backward)
        arrived = [blocks[step] if step in blocks else blocks[step + members] for step in ring_steps]
        fetched = tuple(k for k, step in enumerate(ring_steps) if step in FETCHED.get(index, ()))
        for_near = product(arrived, near_all, fetched)
        from_near = lax.ppermute(for_near, "vir", across)
        rest = product(arrived, kept_all, fetched, base, start)
        raws.append(rest + from_near)

    if cores == 2:
        others = [other_core(raw) for raw in raws]
        index = (mirror_row - occ_place * rows) % (2 * rows)
        if rows % 8 or len(chunks) < 2:
            return add_mirror(index, rows, raws, others)
        ahead = chunks[-1][0]
        late = jnp.concatenate([mirror_row[ahead:], other_core(mirror_row)[ahead:]])
        late = late - occ_place * rows
        target = jnp.where((late >= 0) & (late < rows), late, rows)
        index = jnp.where(index < ahead, index, index - rows + ahead)
        index = jnp.where(index >= 2 * ahead, 0, jnp.maximum(index, 0))
        return add_mirror_in_steps(index, target, rows, raws, others)
    own = jnp.concatenate(raws, axis=0)
    whole = lax.all_gather(own, "occ", axis=0, tiled=True)
    padded = -(-rows // 8) * 8
    own = jnp.pad(own, ((0, padded - rows), (0, 0)))
    return add_mirror(mirror_row + padded, rows, [own], [whole])


def solution(mesh):
    cores, chips = mesh.shape["occ"], mesh.shape["vir"]

    def body(*arrays):
        return shards(cores, chips, *arrays)

    return jax.shard_map(
        body,
        mesh=mesh,
        in_specs=(
            P("occ", "vir"),
            P("vir", "occ"),
            P(),
            P("occ", None),
            P(),
            P("occ", None),
            P("occ"),
        ),
        out_specs=P("occ", "vir"),
        check_vma=False,
    )
```
